128 devices in a mesh: slab: 4 (over y), energy: 32 (over z, x, core).
Axes of the slice: x: 4, y: 4, z: 4, core: 2. Of those that a mesh axis runs over, the one named last changes fastest.
Arguments:
- link_p: float32 [12, 2, 64, 64], P('slab'), may hold values from -1 to 2, as said below
- link_q: float32 [12, 2, 64, 64], P('slab'), may hold values from -1 to 2, as said below
- shift: float32 [64, 12, 64], P('energy', 'slab'), may hold values from 0.01 to 0.3
- lesser_gain: float32 [64, 12, 64], P('energy', 'slab'), may hold values from 0.1 to 2
- sources: float32 [12, 2, 64, 128], P('slab'), may hold values from -1.8 to 1.8
Outputs:
- polar: float32 [2, 64, 12, 64, 128], P(None, None, 'slab', 'energy')
The draws below stay inside these ranges and needn't reach their ends.
Inputs may be any that keep to these rules, and one draw needn't show every extreme that they name: `link_p`: real and imaginary parts of complex link factors. `link_q`: real and imaginary parts of complex link factors.
All inputs are finite; a program needn't handle non-finite values.
Results may differ from the reference program's by a relative error of at most 0.0003.
Values sent between devices are 32-bit elements; how exact they have to be, the bound alone decides.
A program may use at most 64 MiB of HBM per device.

```python
import math
import jax
import jax.numpy as jnp
from jax import lax

ORB = 64
R = 128
NE = 64
NSLAB = 12


def link_factor(key):
    noise = jnp.clip(jax.random.normal(key, (NSLAB, 2, ORB, ORB), jnp.float32), -4.0, 4.0)
    noise = noise * (0.35 / math.sqrt(ORB))
    identity = jnp.eye(ORB, dtype=jnp.float32)
    return noise.at[:, 0].add(identity)


def draw_link_p(key, part):
    return link_factor(jax.random.fold_in(key, 11))


def draw_link_q(key, part):
    return link_factor(jax.random.fold_in(key, 23))


def level_of(key, extent, split, least, top_value):
    loudness = 1.0
    for dim, shards_of in split:
        steps = jax.random.uniform(jax.random.fold_in(jax.random.fold_in(key, 6), dim), (shards_of,), jnp.float32, least / len(split), top_value / len(split))
        loudness = loudness * jnp.repeat(jnp.exp(steps), extent[dim] // shards_of).reshape((-1,) + (1,) * (len(extent) - 1 - dim))
    return loudness


def bell_draw(stream_key, extent, deviation, bound, cuts=(), kind=jnp.bfloat16):
    drawn = jax.random.normal(stream_key, extent, jnp.float32) * deviation
    if len(cuts) > 0:
        drawn = level_of(stream_key, extent, cuts, -0.22, 0.18) * drawn
    return jnp.clip(drawn, min=-bound, max=bound).astype(kind)


def setup_inputs(seed: int = 0) -> dict:
    arg_keys = jax.random.split(jax.random.key(seed), 6)
    link_p = draw_link_p(jax.random.fold_in(arg_keys[5], 71), 0)
    link_q = draw_link_q(jax.random.fold_in(arg_keys[5], 71), 0)
    shift = jnp.clip(jnp.exp(math.log(0.3) - 3.4011974 * jax.random.uniform(arg_keys[2], (NE, NSLAB, ORB), jnp.float32) ** level_of(arg_keys[2], (NE, NSLAB, ORB), ((0, 32), (1, 4)), -0.2, 0.2)), 0.01, 0.3)
    lesser_gain = jnp.clip(jnp.exp(math.log(2.0) - 2.9957323 * jax.random.uniform(arg_keys[3], (NE, NSLAB, ORB), jnp.float32) ** level_of(arg_keys[3], (NE, NSLAB, ORB), ((0, 32), (1, 4)), -0.2, 0.2)), 0.1, 2.0)
    sources = bell_draw(arg_keys[4], (NSLAB, 2, ORB, R), 0.3, 1.8, ((0, 4),), jnp.float32)
    return dict(link_p=link_p, link_q=link_q, shift=shift, lesser_gain=lesser_gain, sources=sources)


HIGHEST = lax.Precision.HIGHEST

def real_form(part):
    real = part[..., 0, :, :]
    imag = part[..., 1, :, :]
    upper_half = jnp.concatenate([real, -imag], axis=-1)
    lower_half = jnp.concatenate([imag, real], axis=-1)
    return jnp.concatenate([upper_half, lower_half], axis=-2)

def right_transposed(left, right):
    return jnp.einsum('...ij,...kj->...ik', left, right, precision=HIGHEST)

def left_transposed(left, right):
    return jnp.einsum('...ji,...jk->...ik', left, right, precision=HIGHEST)

def product(left, right):
    return jnp.einsum('...ij,...jk->...ik', left, right, precision=HIGHEST)

def solve_with(factor, rhs):
    return jax.scipy.linalg.cho_solve((factor, True), rhs)

def chain(diag, upper, sources_flat, gain_row):
    upper_full = jnp.concatenate([upper, jnp.zeros_like(upper[:1])], axis=0)

    def factor_step(carry, pieces):
        block, link_block = pieces
        factor = jnp.linalg.cholesky(block - carry)
        step = solve_with(factor, link_block)
        return (left_transposed(link_block, step), (factor, step))
    unused, stored = lax.scan(factor_step, jnp.zeros_like(diag[0]), (diag, upper_full))
    factors, steps = stored

    def solve(rhs):

        def down(carry, pieces):
            factor, link_block, rhs_row = pieces
            solved = solve_with(factor, rhs_row - carry)
            return (left_transposed(link_block, solved), solved)
        unused_down, partial_rows = lax.scan(down, jnp.zeros_like(rhs[0]), (factors, upper_full, rhs))

        def climb(carry, pieces):
            step, partial_row = pieces
            value = partial_row - product(step, carry)
            return (value, value)
        unused_up, values = lax.scan(climb, jnp.zeros_like(rhs[0]), (steps, partial_rows), reverse=True)
        return values
    retarded = solve(sources_flat)
    lesser = solve(gain_row[..., None] * retarded)
    return (retarded, lesser)

def reference(link_p, link_q, shift, lesser_gain, sources):
    width = 2 * ORB
    rp = real_form(link_p)
    rq = real_form(link_q)
    pp = right_transposed(rp, rp)
    qq = right_transposed(rq, rq)
    cc = -right_transposed(rp, rq)
    base = qq + jnp.concatenate([pp[1:], jnp.zeros_like(pp[:1])], axis=0)
    base = base.at[0].add(pp[0])
    upper = cc[1:]
    eye = jnp.eye(width, dtype=jnp.float32)
    shift_two = jnp.concatenate([shift, shift], axis=-1)
    gain_two = jnp.concatenate([lesser_gain, lesser_gain], axis=-1)
    sources_flat = sources.reshape(NSLAB, width, R)

    def per_energy(pieces):
        shift_row, gain_row = pieces
        diag = base + eye * shift_row[:, None, :]
        retarded, lesser = chain(diag, upper, sources_flat, gain_row)
        ret_real = retarded[:, :ORB]
        ret_imag = retarded[:, ORB:]
        les_real = lesser[:, :ORB]
        les_imag = lesser[:, ORB:]
        return (ret_real * les_real + ret_imag * les_imag, ret_real * les_imag - ret_imag * les_real, ret_real * ret_real + ret_imag * ret_imag)
    lesser_re, lesser_im, power = lax.map(per_energy, (shift_two, gain_two))
    padded_re = jnp.concatenate([lesser_re, jnp.zeros_like(lesser_re)], axis=0)
    padded_im = jnp.concatenate([lesser_im, jnp.zeros_like(lesser_im)], axis=0)

    def lag(offset):
        part_re = lax.dynamic_slice_in_dim(padded_re, offset, NE, 0)
        part_im = lax.dynamic_slice_in_dim(padded_im, offset, NE, 0)
        return (jnp.sum(part_re * power, axis=0), jnp.sum(part_im * power, axis=0))
    corr_re, corr_im = lax.map(lag, jnp.arange(NE, dtype=jnp.int32))
    return jnp.stack([corr_re, corr_im], axis=0) / NE
```

```python
import functools

import jax
import jax.numpy as jnp
from jax import lax
from jax.experimental import pallas as pl
from jax.experimental.pallas import tpu as pltpu
from jax.sharding import PartitionSpec as P

HIGHEST = lax.Precision.HIGHEST
F32 = jnp.float32
ORB = 64
LANES = 128
SLABS = 12
LEVELS = (
    ((0, None, 1), (2, 1, 3), (4, 3, 5), (6, 5, 7), (8, 7, 9), (10, 9, 11)),
    ((1, None, 3), (5, 3, 7), (9, 7, 11)),
    ((3, None, 7), (11, 7, None)),
    ((7, None, None),),
)
STEPS = {6: 1, 3: 2, 2: 2, 1: 4}


def lane_of(shape):
    return lax.broadcasted_iota(jnp.int32, shape, len(shape) - 1)


def row_of(shape):
    return lax.broadcasted_iota(jnp.int32, shape, len(shape) - 2)


def times_i(value):
    turned = pltpu.roll(value, ORB, 1)
    return jnp.where(lane_of(value.shape) < ORB, -turned, turned)


def right_form(value):
    return jnp.concatenate([value, times_i(value)], axis=0)


def dot(left, right):
    return jnp.dot(left, right, precision=HIGHEST, preferred_element_type=F32)


def pivot_inverse(diag, cross, size):
    if size == 1:
        return [[(1.0 / diag[0], None)]]
    if size == 2:
        re, im = cross[0, 1]
        scale = 1.0 / (diag[0] * diag[1] - re * re - im * im)
        re, im = re * scale, im * scale
        return [[(diag[1] * scale, None), (-re, -im)], [(-re, im), (diag[0] * scale, None)]]
    held = {(i, i): (diag[i], None) for i in range(size)}
    held.update(cross)

    def entry(i, j):
        if i <= j:
            return held[i, j]
        return (held[j, i][0], -held[j, i][1])

    for p in range(size):
        inverse = 1.0 / held[p, p][0]
        row = {j: entry(p, j) for j in range(size) if j != p}
        scaled = {j: (row[j][0] * inverse, row[j][1] * inverse) for j in row}
        after = {(p, p): (-inverse, None)}
        for i in row:
            for j in row:
                if i > j:
                    continue
                real = held[i, j][0] - row[i][0] * scaled[j][0] - row[i][1] * scaled[j][1]
                imag = None
                if i != j:
                    imag = held[i, j][1] - row[i][0] * scaled[j][1] + row[i][1] * scaled[j][0]
                after[i, j] = (real, imag)
        for j in row:
            if p < j:
                after[p, j] = scaled[j]
            else:
                after[j, p] = (scaled[j][0], -scaled[j][1])
        held = after
    out = []
    for i in range(size):
        out.append([])
        for j in range(size):
            real, imag = entry(i, j) if i != j else held[i, i]
            out[i].append((-real, None if imag is None else -imag))
    return out


def invert_all(values, size):
    lanes = lane_of((1, LANES))
    rows = row_of((ORB, LANES))
    zero = jnp.zeros((1, LANES), F32)
    for k in range(0, ORB, size):
        later = []
        for value in values:
            tops = [value[k + j : k + j + 1, :] for j in range(size)]
            turned = [times_i(top) for top in tops]
            cols = []
            for j in range(size):
                at = k + j
                cols.append(
                    (
                        jnp.broadcast_to(value[:, at : at + 1], (ORB, LANES)),
                        jnp.broadcast_to(value[:, ORB + at : ORB + at + 1], (ORB, LANES)),
                    )
                )
            diag = [cols[j][0][k + j : k + j + 1] for j in range(size)]
            cross = {}
            for i in range(size):
                for j in range(i + 1, size):
                    cross[i, j] = (cols[j][0][k + i : k + i + 1], cols[j][1][k + i : k + i + 1])
            small = pivot_inverse(diag, cross, size)
            fresh = []
            for i in range(size):
                plain = zero
                rotated = zero
                for j in range(size):
                    real, imag = small[i][j]
                    plain = plain + real * tops[j]
                    rotated = rotated + real * turned[j]
                    if imag is not None:
                        plain = plain + imag * turned[j]
                        rotated = rotated - imag * tops[j]
                for j in range(size):
                    real, imag = small[i][j]
                    imag = zero if imag is None else imag
                    on_real, on_imag = lanes == k + j, lanes == ORB + k + j
                    plain = jnp.where(on_real, real, jnp.where(on_imag, imag, plain))
                    rotated = jnp.where(on_real, -imag, jnp.where(on_imag, real, rotated))
                fresh.append((plain, rotated))
            inside = lanes & (ORB - 1)
            inside = (inside >= k) & (inside < k + size)
            total = jnp.where(inside, 0.0, value)
            for j in range(size):
                total = total - cols[j][0] * fresh[j][0] - cols[j][1] * fresh[j][1]
            for j in range(size):
                total = jnp.where(rows == k + j, fresh[j][0], total)
            later.append(total)
        values = later
    return values


def solve_kernel(p_ref, q_ref, src_ref, shift_ref, gain_ref, out_ref, diag, link, inv, rhs, sol):
    slot = {}

    def at(i, j):
        return slot.setdefault((i, j), len(slot))

    corner = lane_of((ORB, LANES)) == row_of((ORB, LANES))
    for s in range(SLABS):
        p, q = p_ref[s], q_ref[s]
        left = jnp.concatenate([p, q], axis=0)
        right = jnp.concatenate([p, times_i(p), q, times_i(q)], axis=0)
        both = lax.dot_general(
            left, right, (((1,), (1,)), ((), ())), precision=HIGHEST, preferred_element_type=F32
        )
        own = both[ORB:, LANES:]
        before = both[:ORB, :LANES]
        shift = jnp.broadcast_to(shift_ref[s : s + 1, :], (ORB, LANES))
        own = own + jnp.where(corner, shift, 0.0)
        if s == 0:
            diag[s] = own + before
        else:
            diag[s] = own
            diag[s - 1] = diag[s - 1] + before
            link[at(s - 1, s)] = -both[:ORB, LANES:]
            link[at(s, s - 1)] = -both[ORB:, :LANES]
        rhs[s] = src_ref[s]

    plan = []
    for level in LEVELS:
        inverses = invert_all([diag[s] for s, _, _ in level], STEPS[len(level)])
        for (s, l, r), inverse in zip(level, inverses):
            inv[s] = inverse
        updates = []
        for s, l, r in level:
            near = [n for n in (l, r) if n is not None]
            sides = [right_form(link[at(s, n)]) for n in near] + [right_form(rhs[s])]
            step = dot(inv[s], jnp.concatenate(sides, axis=1))
            rhs[s] = step[:, LANES * len(near) :]
            if not near:
                continue
            back = jnp.concatenate([link[at(n, s)] for n in near], axis=0)
            pieces = [step[:, LANES * i : LANES * (i + 1)] for i in range(len(near) + 1)]
            moved = dot(back, jnp.concatenate([right_form(piece) for piece in pieces], axis=1))
            for i, n in enumerate(near):
                link[at(s, n)] = pieces[i]
                for j, m in enumerate(near):
                    block = moved[ORB * i : ORB * (i + 1), LANES * j : LANES * (j + 1)]
                    if n == m:
                        diag[n] = diag[n] - block
                    else:
                        link[at(n, m)] = -block
                rhs[n] = rhs[n] - moved[ORB * i : ORB * (i + 1), LANES * len(near) :]

    def climb():
        for level in reversed(LEVELS):
            for s, l, r in level:
                near = [n for n in (l, r) if n is not None]
                if not near:
                    sol[s] = rhs[s]
                    continue
                steps = jnp.concatenate([link[at(s, n)] for n in near], axis=1)
                values = jnp.concatenate([right_form(sol[n]) for n in near], axis=0)
                sol[s] = rhs[s] - dot(steps, values)

    climb()
    for s in range(SLABS):
        gain = jnp.sum(
            jnp.where(corner, jnp.broadcast_to(gain_ref[s : s + 1, :], (ORB, LANES)), 0.0),
            axis=1,
            keepdims=True,
        )
        diag[s] = sol[s]
        rhs[s] = gain * sol[s]
    for level in LEVELS:
        for s, l, r in level:
            near = [n for n in (l, r) if n is not None]
            step = dot(inv[s], right_form(rhs[s]))
            rhs[s] = step
            if not near:
                continue
            back = jnp.concatenate([link[at(n, s)] for n in near], axis=0)
            moved = dot(back, right_form(step))
            for i, n in enumerate(near):
                rhs[n] = rhs[n] - moved[ORB * i : ORB * (i + 1)]
    climb()
    first = lane_of((ORB, LANES)) < ORB
    for s in range(SLABS):
        x, y = diag[s], sol[s]
        x_turned = pltpu.roll(x, ORB, 1)
        y_turned = pltpu.roll(y, ORB, 1)
        same = x * y
        crossed = x_turned * y
        pair = jnp.where(first, same + pltpu.roll(same, ORB, 1), crossed - x * y_turned)
        square = x * x
        power = square + pltpu.roll(square, ORB, 1)
        inv[s] = pair
        link[s] = power
        base = (s // 3) * (32 * 9) + (s % 3) * 3
        even = link[s, pl.ds(0, 32, stride=2), :]
        odd = link[s, pl.ds(1, 32, stride=2), :]
        out_ref[pl.ds(base, 32, stride=9), :] = inv[s, pl.ds(0, 32, stride=2), :]
        out_ref[pl.ds(base + 1, 32, stride=9), :] = inv[s, pl.ds(1, 32, stride=2), :]
        out_ref[pl.ds(base + 2, 32, stride=9), :] = jnp.where(lane_of((32, LANES)) < ORB, even, odd)


def solve_all(p, q, src, shift, gain):
    return pl.pallas_call(
        solve_kernel,
        out_shape=jax.ShapeDtypeStruct((SLABS * 96, LANES), F32),
        in_specs=[pl.BlockSpec(memory_space=pltpu.VMEM)] * 5,
        out_specs=pl.BlockSpec(memory_space=pltpu.VMEM),
        scratch_shapes=[
            pltpu.VMEM((SLABS, ORB, LANES), F32),
            pltpu.VMEM((44, ORB, LANES), F32),
            pltpu.VMEM((SLABS, ORB, LANES), F32),
            pltpu.VMEM((SLABS, ORB, LANES), F32),
            pltpu.VMEM((SLABS, ORB, LANES), F32),
        ],
        compiler_params=pltpu.CompilerParams(vmem_limit_bytes=48 << 20),
        name="solve",
    )(p, q, src, shift, gain)


ENERGIES = 64


def lag_kernel(in_ref, out_ref, gl, gg):
    first = lane_of((ENERGIES, LANES)) < ORB
    for half in range(2):
        gl[half, pl.ds(ENERGIES, 8), :] = jnp.zeros((8, LANES), F32)

    def one(index, unused):
        slab = index // 2
        orbital = index % 2
        sums = []
        for half in range(2):
            for parity in range(2):
                base = (half * 2 + parity) * (32 * 9) + slab * 3
                gl[half, pl.ds(parity, 32, stride=2), :] = in_ref[
                    pl.ds(base + orbital, 32, stride=9), :
                ]
                gg[half, pl.ds(parity, 32, stride=2), :] = in_ref[pl.ds(base + 2, 32, stride=9), :]
            power = gg[half]
            turned = pltpu.roll(power, ORB, 1)
            low = jnp.where(first, power, turned)
            high = jnp.where(first, turned, power)
            gg[half] = jnp.where(orbital == 0, low, high)
            acc = [jnp.zeros((8, LANES), F32) for _ in range(8)]
            for energy in range(ENERGIES):
                weight = jnp.broadcast_to(gg[half, energy : energy + 1, :], (8, LANES))
                for block in range((ENERGIES - energy + 7) // 8):
                    acc[block] = acc[block] + weight * gl[half, pl.ds(energy + 8 * block, 8), :]
            sums.append(jnp.concatenate(acc, axis=0))
        zero_turned = pltpu.roll(sums[0], ORB, 1)
        one_turned = pltpu.roll(sums[1], ORB, 1)
        scale = 1.0 / ENERGIES
        out_ref[pl.ds(index, ENERGIES, stride=6), :] = jnp.where(first, sums[0], one_turned) * scale
        out_ref[pl.ds(ENERGIES * 6 + index, ENERGIES, stride=6), :] = (
            jnp.where(first, zero_turned, sums[1]) * scale
        )
        return unused

    lax.fori_loop(0, 6, one, 0)


def correlate(received):
    return pl.pallas_call(
        lag_kernel,
        out_shape=jax.ShapeDtypeStruct((2 * ENERGIES * 6, LANES), F32),
        in_specs=[pl.BlockSpec(memory_space=pltpu.VMEM)],
        out_specs=pl.BlockSpec(memory_space=pltpu.VMEM),
        scratch_shapes=[
            pltpu.VMEM((2, ENERGIES + 8, LANES), F32),
            pltpu.VMEM((2, ENERGIES, LANES), F32),
        ],
        compiler_params=pltpu.CompilerParams(vmem_limit_bytes=32 << 20),
        name="lags",
    )(received)


def row_layout(parts):
    return jnp.concatenate([parts[:, 0], parts[:, 1]], axis=-1)


def per_device(link_p, link_q, shift, lesser_gain, sources):
    group = lax.axis_index("slab")
    halves = [row_layout(sources[..., :ORB]), row_layout(sources[..., ORB:])]
    packed = jnp.stack([row_layout(link_p), row_layout(link_q)] + halves, axis=0)
    packed = lax.all_gather(packed, "slab", axis=1, tiled=True)
    small = jnp.concatenate([shift, lesser_gain], axis=-1)
    small = lax.all_gather(small, "slab", axis=1, tiled=True)
    mine = lax.dynamic_index_in_dim(small, group % 2, 0, keepdims=False)
    src = lax.dynamic_index_in_dim(packed, 2 + group // 2, 0, keepdims=False)
    gain = jnp.concatenate([mine[:, ORB:], mine[:, :ORB]], axis=-1)
    sent = solve_all(packed[0], packed[1], src, mine, gain)
    sent = sent.reshape(4 * 32, 9, LANES)
    received = lax.all_to_all(sent, ("slab", "energy"), split_axis=0, concat_axis=0, tiled=True)
    out = correlate(received.reshape(SLABS * 96, LANES))
    return out.reshape(2, ENERGIES, 3, 2, LANES)


def solution(mesh):
    placed = (
        P("slab", None, None, None),
        P("slab", None, None, None),
        P("energy", "slab", None),
        P("energy", "slab", None),
        P("slab", None, None, None),
    )
    return jax.shard_map(
        per_device,
        mesh=mesh,
        in_specs=placed,
        out_specs=P(None, None, "slab", "energy", None),
        check_vma=False,
    )
```

```python
import functools

import jax
import jax.numpy as jnp
from jax import lax
from jax.experimental import pallas as pl
from jax.experimental.pallas import tpu as pltpu
from jax.sharding import PartitionSpec as P

HIGHEST = lax.Precision.HIGHEST
F32 = jnp.float32
ORB = 64
LANES = 128
SLABS = 12
LEVELS = (
    ((0, None, 1), (2, 1, 3), (4, 3, 5), (6, 5, 7), (8, 7, 9), (10, 9, 11)),
    ((1, None, 3), (5, 3, 7), (9, 7, 11)),
    ((3, None, 7), (11, 7, None)),
    ((7, None, None),),
)
STEPS = {6: 1, 3: 2, 2: 2, 1: 4}


def lane_of(shape):
    return lax.broadcasted_iota(jnp.int32, shape, len(shape) - 1)


def row_of(shape):
    return lax.broadcasted_iota(jnp.int32, shape, len(shape) - 2)


def times_i(value):
    turned = pltpu.roll(value, ORB, 1)
    return jnp.where(lane_of(value.shape) < ORB, -turned, turned)


def right_form(value):
    return jnp.concatenate([value, times_i(value)], axis=0)


def dot(left, right):
    return jnp.dot(left, right, precision=HIGHEST, preferred_element_type=F32)


def pivot_inverse(diag, cross, size):
    if size == 1:
        return [[(1.0 / diag[0], None)]]
    if size == 2:
        re, im = cross[0, 1]
        scale = 1.0 / (diag[0] * diag[1] - re * re - im * im)
        re, im = re * scale, im * scale
        return [[(diag[1] * scale, None), (-re, -im)], [(-re, im), (diag[0] * scale, None)]]
    held = {(i, i): (diag[i], None) for i in range(size)}
    held.update(cross)

    def entry(i, j):
        if i <= j:
            return held[i, j]
        return (held[j, i][0], -held[j, i][1])

    for p in range(size):
        inverse = 1.0 / held[p, p][0]
        row = {j: entry(p, j) for j in range(size) if j != p}
        scaled = {j: (row[j][0] * inverse, row[j][1] * inverse) for j in row}
        after = {(p, p): (-inverse, None)}
        for i in row:
            for j in row:
                if i > j:
                    continue
                real = held[i, j][0] - row[i][0] * scaled[j][0] - row[i][1] * scaled[j][1]
                imag = None
                if i != j:
                    imag = held[i, j][1] - row[i][0] * scaled[j][1] + row[i][1] * scaled[j][0]
                after[i, j] = (real, imag)
        for j in row:
            if p < j:
                after[p, j] = scaled[j]
            else:
                after[j, p] = (scaled[j][0], -scaled[j][1])
        held = after
    out = []
    for i in range(size):
        out.append([])
        for j in range(size):
            real, imag = entry(i, j) if i != j else held[i, i]
            out[i].append((-real, None if imag is None else -imag))
    return out


def invert_all(values, size):
    lanes = lane_of((1, LANES))
    rows = row_of((ORB, LANES))
    zero = jnp.zeros((1, LANES), F32)
    for k in range(0, ORB, size):
        later = []
        for value in values:
            tops = [value[k + j : k + j + 1, :] for j in range(size)]
            turned = [times_i(top) for top in tops]
            cols = []
            for j in range(size):
                at = k + j
                cols.append(
                    (
                        jnp.broadcast_to(value[:, at : at + 1], (ORB, LANES)),
                        jnp.broadcast_to(value[:, ORB + at : ORB + at + 1], (ORB, LANES)),
                    )
                )
            diag = [cols[j][0][k + j : k + j + 1] for j in range(size)]
            cross = {}
            for i in range(size):
                for j in range(i + 1, size):
                    cross[i, j] = (cols[j][0][k + i : k + i + 1], cols[j][1][k + i : k + i + 1])
            small = pivot_inverse(diag, cross, size)
            fresh = []
            for i in range(size):
                plain = zero
                rotated = zero
                for j in range(size):
                    real, imag = small[i][j]
                    plain = plain + real * tops[j]
                    rotated = rotated + real * turned[j]
                    if imag is not None:
                        plain = plain + imag * turned[j]
                        rotated = rotated - imag * tops[j]
                for j in range(size):
                    real, imag = small[i][j]
                    imag = zero if imag is None else imag
                    on_real, on_imag = lanes == k + j, lanes == ORB + k + j
                    plain = jnp.where(on_real, real, jnp.where(on_imag, imag, plain))
                    rotated = jnp.where(on_real, -imag, jnp.where(on_imag, real, rotated))
                fresh.append((plain, rotated))
            inside = lanes & (ORB - 1)
            inside = (inside >= k) & (inside < k + size)
            total = jnp.where(inside, 0.0, value)
            for j in range(size):
                total = total - cols[j][0] * fresh[j][0] - cols[j][1] * fresh[j][1]
            for j in range(size):
                total = jnp.where(rows == k + j, fresh[j][0], total)
            later.append(total)
        values = later
    return values


def solve_kernel(in_ref, small_ref, out_ref, diag, link, inv, rhs, sol):
    slot = {}

    def at(i, j):
        return slot.setdefault((i, j), len(slot))

    corner = lane_of((ORB, LANES)) == row_of((ORB, LANES))
    far_corner = lane_of((ORB, LANES)) == row_of((ORB, LANES)) + ORB
    for s in range(SLABS):
        group, i = divmod(s, 3)
        p = in_ref[group, 0, i * ORB : (i + 1) * ORB, :]
        q = in_ref[group, 1, i * ORB : (i + 1) * ORB, :]
        left = jnp.concatenate([p, q], axis=0)
        right = jnp.concatenate([p, times_i(p), q, times_i(q)], axis=0)
        both = lax.dot_general(
            left, right, (((1,), (1,)), ((), ())), precision=HIGHEST, preferred_element_type=F32
        )
        own = both[ORB:, LANES:]
        before = both[:ORB, :LANES]
        shift = jnp.broadcast_to(small_ref[group, i : i + 1, :], (ORB, LANES))
        own = own + jnp.where(corner, shift, 0.0)
        if s == 0:
            diag[s] = own + before
        else:
            diag[s] = own
            diag[s - 1] = diag[s - 1] + before
            link[at(s - 1, s)] = -both[:ORB, LANES:]
            link[at(s, s - 1)] = -both[ORB:, :LANES]
        for part in range(2):
            side, offset = divmod(i * ORB + part * 32, HALF_ROWS)
            rhs[s, part * 32 : part * 32 + 32, :] = in_ref[
                group, side, LINK_ROWS + offset : LINK_ROWS + offset + 32, :
            ]

    plan = []
    for level in LEVELS:
        inverses = invert_all([diag[s] for s, _, _ in level], STEPS[len(level)])
        for (s, l, r), inverse in zip(level, inverses):
            inv[s] = inverse
        updates = []
        for s, l, r in level:
            near = [n for n in (l, r) if n is not None]
            sides = [right_form(link[at(s, n)]) for n in near] + [right_form(rhs[s])]
            step = dot(inv[s], jnp.concatenate(sides, axis=1))
            rhs[s] = step[:, LANES * len(near) :]
            if not near:
                continue
            back = jnp.concatenate([link[at(n, s)] for n in near], axis=0)
            pieces = [step[:, LANES * i : LANES * (i + 1)] for i in range(len(near) + 1)]
            moved = dot(back, jnp.concatenate([right_form(piece) for piece in pieces], axis=1))
            for i, n in enumerate(near):
                link[at(s, n)] = pieces[i]
                for j, m in enumerate(near):
                    block = moved[ORB * i : ORB * (i + 1), LANES * j : LANES * (j + 1)]
                    if n == m:
                        diag[n] = diag[n] - block
                    else:
                        link[at(n, m)] = -block
                rhs[n] = rhs[n] - moved[ORB * i : ORB * (i + 1), LANES * len(near) :]

    def climb():
        for level in reversed(LEVELS):
            for s, l, r in level:
                near = [n for n in (l, r) if n is not None]
                if not near:
                    sol[s] = rhs[s]
                    continue
                steps = jnp.concatenate([link[at(s, n)] for n in near], axis=1)
                values = jnp.concatenate([right_form(sol[n]) for n in near], axis=0)
                sol[s] = rhs[s] - dot(steps, values)

    climb()
    for s in range(SLABS):
        gain = jnp.sum(
            jnp.where(
                far_corner,
                jnp.broadcast_to(small_ref[s // 3, s % 3 : s % 3 + 1, :], (ORB, LANES)),
                0.0,
            ),
            axis=1,
            keepdims=True,
        )
        diag[s] = sol[s]
        rhs[s] = gain * sol[s]
    for level in LEVELS:
        for s, l, r in level:
            near = [n for n in (l, r) if n is not None]
            step = dot(inv[s], right_form(rhs[s]))
            rhs[s] = step
            if not near:
                continue
            back = jnp.concatenate([link[at(n, s)] for n in near], axis=0)
            moved = dot(back, right_form(step))
            for i, n in enumerate(near):
                rhs[n] = rhs[n] - moved[ORB * i : ORB * (i + 1)]
    climb()
    first = lane_of((ORB, LANES)) < ORB
    for s in range(SLABS):
        x, y = diag[s], sol[s]
        x_turned = pltpu.roll(x, ORB, 1)
        y_turned = pltpu.roll(y, ORB, 1)
        same = x * y
        crossed = x_turned * y
        pair = jnp.where(first, same + pltpu.roll(same, ORB, 1), crossed - x * y_turned)
        square = x * x
        power = square + pltpu.roll(square, ORB, 1)
        inv[s] = pair
        link[s] = power
        base = (s // 3) * (32 * 9) + (s % 3) * 3
        even = link[s, pl.ds(0, 32, stride=2), :]
        odd = link[s, pl.ds(1, 32, stride=2), :]
        out_ref[pl.ds(base, 32, stride=9), :] = inv[s, pl.ds(0, 32, stride=2), :]
        out_ref[pl.ds(base + 1, 32, stride=9), :] = inv[s, pl.ds(1, 32, stride=2), :]
        out_ref[pl.ds(base + 2, 32, stride=9), :] = jnp.where(lane_of((32, LANES)) < ORB, even, odd)


def solve_all(gathered, small):
    return pl.pallas_call(
        solve_kernel,
        out_shape=jax.ShapeDtypeStruct((SLABS * 96, LANES), F32),
        in_specs=[pl.BlockSpec(memory_space=pltpu.VMEM)] * 2,
        out_specs=pl.BlockSpec(memory_space=pltpu.VMEM),
        scratch_shapes=[
            pltpu.VMEM((SLABS, ORB, LANES), F32),
            pltpu.VMEM((44, ORB, LANES), F32),
            pltpu.VMEM((SLABS, ORB, LANES), F32),
            pltpu.VMEM((SLABS, ORB, LANES), F32),
            pltpu.VMEM((SLABS, ORB, LANES), F32),
        ],
        compiler_params=pltpu.CompilerParams(vmem_limit_bytes=48 << 20),
        name="solve",
    )(gathered, small)


ENERGIES = 64


def lag_kernel(in_ref, out_ref, gl, gg):
    first = lane_of((ENERGIES, LANES)) < ORB
    for half in range(2):
        gl[half, pl.ds(ENERGIES, 8), :] = jnp.zeros((8, LANES), F32)

    def one(index, unused):
        slab = index // 2
        orbital = index % 2
        sums = []
        for half in range(2):
            for parity in range(2):
                base = (half * 2 + parity) * (32 * 9) + slab * 3
                gl[half, pl.ds(parity, 32, stride=2), :] = in_ref[
                    pl.ds(base + orbital, 32, stride=9), :
                ]
                gg[half, pl.ds(parity, 32, stride=2), :] = in_ref[pl.ds(base + 2, 32, stride=9), :]
            power = gg[half]
            turned = pltpu.roll(power, ORB, 1)
            low = jnp.where(first, power, turned)
            high = jnp.where(first, turned, power)
            gg[half] = jnp.where(orbital == 0, low, high)
            acc = [jnp.zeros((8, LANES), F32) for _ in range(8)]
            for energy in range(ENERGIES):
                weight = jnp.broadcast_to(gg[half, energy : energy + 1, :], (8, LANES))
                for block in range((ENERGIES - energy + 7) // 8):
                    acc[block] = acc[block] + weight * gl[half, pl.ds(energy + 8 * block, 8), :]
            sums.append(jnp.concatenate(acc, axis=0))
        zero_turned = pltpu.roll(sums[0], ORB, 1)
        one_turned = pltpu.roll(sums[1], ORB, 1)
        scale = 1.0 / ENERGIES
        out_ref[pl.ds(index, ENERGIES, stride=6), :] = jnp.where(first, sums[0], one_turned) * scale
        out_ref[pl.ds(ENERGIES * 6 + index, ENERGIES, stride=6), :] = (
            jnp.where(first, zero_turned, sums[1]) * scale
        )
        return unused

    lax.fori_loop(0, 6, one, 0)


def correlate(received):
    return pl.pallas_call(
        lag_kernel,
        out_shape=jax.ShapeDtypeStruct((2 * ENERGIES * 6, LANES), F32),
        in_specs=[pl.BlockSpec(memory_space=pltpu.VMEM)],
        out_specs=pl.BlockSpec(memory_space=pltpu.VMEM),
        scratch_shapes=[
            pltpu.VMEM((2, ENERGIES + 8, LANES), F32),
            pltpu.VMEM((2, ENERGIES, LANES), F32),
        ],
        compiler_params=pltpu.CompilerParams(vmem_limit_bytes=32 << 20),
        name="lags",
    )(received)


GROUPS = 4
PER_GROUP = 32
LINK_ROWS = 3 * ORB
HALF_ROWS = LINK_ROWS // 2
PIECE_ROWS = LINK_ROWS + HALF_ROWS
CHUNKS = ((0, LINK_ROWS), (LINK_ROWS, HALF_ROWS))
MESH = pl.DeviceIdType.MESH


def gather_kernel(
    p_ref, q_ref, shift_ref, gain_ref, src_ref, out_ref, small_ref,
    piece, small_piece, sent, arrived, passed, handed, small_sent, small_arrived,
):
    group = lax.axis_index("slab")
    spot = lax.axis_index("energy")
    core = lax.rem(spot, 2)
    sibling = spot + 1 - 2 * core
    barrier = pltpu.get_barrier_semaphore()
    for d in range(1, GROUPS):
        pl.semaphore_signal(
            barrier, inc=1, device_id=(lax.rem(group + d, GROUPS), spot), device_id_type=MESH
        )
    pl.semaphore_signal(barrier, inc=1, device_id=(group, sibling), device_id_type=MESH)
    my_half = group // 2

    def rows_of(part):
        return jnp.concatenate([part[0], part[1]], axis=1)

    for i in range(3):
        p, q = rows_of(p_ref[i]), rows_of(q_ref[i])
        span = pl.ds(i * ORB, ORB)
        out_ref[group, 0, span, :] = p
        out_ref[group, 1, span, :] = q
        mine = jnp.where(core == 0, p, q)
        piece[0, span, :] = mine
        piece[1, span, :] = mine
        real, imag = src_ref[i, 0], src_ref[i, 1]
        first = lane_of((ORB, LANES)) < ORB
        halves = (
            jnp.where(first, real, pltpu.roll(imag, ORB, 1)),
            jnp.where(first, pltpu.roll(real, ORB, 1), imag),
        )
        own = jnp.where(my_half == 0, halves[0], halves[1])
        for part in range(2):
            low = i * ORB + part * 32
            side, offset = divmod(low, HALF_ROWS)
            there = pl.ds(LINK_ROWS + offset, 32)
            rows = slice(part * 32, part * 32 + 32)
            out_ref[group, side, there, :] = own[rows]

            @pl.when(core == side)
            def _():
                piece[0, there, :] = halves[0][rows]
                piece[1, there, :] = halves[1][rows]

    pair = jnp.concatenate([shift_ref[...], gain_ref[...]], axis=-1)
    for parity in range(2):
        small_piece[parity, 0:3, :] = pair[parity]
    small_ref[group, 0:3, :] = jnp.where(lax.rem(group, 2) == 0, pair[0], pair[1])

    pl.semaphore_wait(barrier, GROUPS)
    copies = []
    smalls = []
    for d in (2, 1, 3):
        there = lax.rem(group + d, GROUPS)
        small = pltpu.make_async_remote_copy(
            src_ref=small_piece.at[lax.rem(there, 2)],
            dst_ref=small_ref.at[group],
            send_sem=small_sent.at[d],
            recv_sem=small_arrived.at[d],
            device_id=(there, spot),
            device_id_type=MESH,
        )
        small.start()
        smalls.append(small)
    for c, (low, rows) in enumerate(CHUNKS):
        for d in (2, 1, 3):
            there = lax.rem(group + d, GROUPS)
            copy = pltpu.make_async_remote_copy(
                src_ref=piece.at[there // 2, pl.ds(low, rows)],
                dst_ref=out_ref.at[group, core, pl.ds(low, rows)],
                send_sem=sent.at[c, d],
                recv_sem=arrived.at[c, d],
                device_id=(there, spot),
                device_id_type=MESH,
            )
            copy.start()
            copies.append((c, low, rows, d, copy))
    forwards = []
    for c, low, rows, d, copy in sorted(copies, key=lambda item: (item[0], (1, 3, 2).index(item[3]))):
        copy.wait_recv()
        source = lax.rem(group + GROUPS - d, GROUPS)
        forward = pltpu.make_async_remote_copy(
            src_ref=out_ref.at[source, core, pl.ds(low, rows)],
            dst_ref=out_ref.at[source, core, pl.ds(low, rows)],
            send_sem=passed.at[c, d],
            recv_sem=handed.at[c, d],
            device_id=(group, sibling),
            device_id_type=MESH,
        )
        forward.start()
        forwards.append(forward)
    for small in smalls:
        small.wait()
    for c, low, rows, d, copy in copies:
        copy.wait_send()
    for forward in forwards:
        forward.wait()


def gather_links(link_p, link_q, shift, gain, sources):
    dma = pltpu.SemaphoreType.DMA
    return pl.pallas_call(
        gather_kernel,
        out_shape=(
            jax.ShapeDtypeStruct((GROUPS, 2, PIECE_ROWS, LANES), F32),
            jax.ShapeDtypeStruct((GROUPS, 8, LANES), F32),
        ),
        in_specs=[pl.BlockSpec(memory_space=pltpu.VMEM)] * 5,
        out_specs=[pl.BlockSpec(memory_space=pltpu.VMEM)] * 2,
        scratch_shapes=[
            pltpu.VMEM((2, PIECE_ROWS, LANES), F32),
            pltpu.VMEM((2, 8, LANES), F32),
            dma((2, GROUPS)),
            dma((2, GROUPS)),
            dma((2, GROUPS)),
            dma((2, GROUPS)),
            dma((GROUPS,)),
            dma((GROUPS,)),
        ],
        compiler_params=pltpu.CompilerParams(
            collective_id=0, has_side_effects=True, vmem_limit_bytes=16 << 20
        ),
        name="gather_links",
    )(link_p, link_q, shift, gain, sources)


def exchange_kernel(in_ref, out_ref, sent, arrived, local):
    group = lax.axis_index("slab")
    spot = lax.axis_index("energy")
    here = group * PER_GROUP + spot
    count = GROUPS * PER_GROUP
    barrier = pltpu.get_barrier_semaphore()

    def greet(d, unused):
        there = lax.rem(here + d, count)
        pl.semaphore_signal(
            barrier,
            inc=1,
            device_id=(there // PER_GROUP, lax.rem(there, PER_GROUP)),
            device_id_type=MESH,
        )
        return unused

    lax.fori_loop(1, count, greet, 0)
    own = pltpu.make_async_copy(in_ref.at[here], out_ref.at[here], local)
    own.start()
    pl.semaphore_wait(barrier, count - 1)

    def send(d, unused):
        there = lax.rem(here + d, count)
        pltpu.make_async_remote_copy(
            src_ref=in_ref.at[there],
            dst_ref=out_ref.at[here],
            send_sem=sent,
            recv_sem=arrived,
            device_id=(there // PER_GROUP, lax.rem(there, PER_GROUP)),
            device_id_type=MESH,
        ).start()
        return unused

    lax.fori_loop(1, count, send, 0)
    own.wait()
    others = pl.ds(0, count - 1)
    pltpu.make_async_copy(in_ref.at[others], in_ref.at[others], sent).wait()
    pltpu.make_async_copy(out_ref.at[others], out_ref.at[others], arrived).wait()


def exchange(blocks):
    return pl.pallas_call(
        exchange_kernel,
        out_shape=jax.ShapeDtypeStruct(blocks.shape, F32),
        in_specs=[pl.BlockSpec(memory_space=pltpu.VMEM)],
        out_specs=pl.BlockSpec(memory_space=pltpu.VMEM),
        scratch_shapes=[pltpu.SemaphoreType.DMA, pltpu.SemaphoreType.DMA, pltpu.SemaphoreType.DMA],
        compiler_params=pltpu.CompilerParams(
            collective_id=1, has_side_effects=True, vmem_limit_bytes=16 << 20
        ),
        name="exchange",
    )(blocks)


def per_device(link_p, link_q, shift, lesser_gain, sources):
    gathered, small = gather_links(link_p, link_q, shift, lesser_gain, sources)
    sent = solve_all(gathered, small)
    received = exchange(sent.reshape(GROUPS * PER_GROUP, 9, 1, LANES))
    out = correlate(received.reshape(SLABS * 96, LANES))
    return out.reshape(2, ENERGIES, 3, 2, LANES)


def solution(mesh):
    placed = (
        P("slab", None, None, None),
        P("slab", None, None, None),
        P("energy", "slab", None),
        P("energy", "slab", None),
        P("slab", None, None, None),
    )
    return jax.shard_map(
        per_device,
        mesh=mesh,
        in_specs=placed,
        out_specs=P(None, None, "slab", "energy", None),
        check_vma=False,
    )
```

```python
import functools

import jax
import jax.numpy as jnp
from jax import lax
from jax.experimental import pallas as pl
from jax.experimental.pallas import tpu as pltpu
from jax.sharding import PartitionSpec as P

HIGHEST = lax.Precision.HIGHEST
F32 = jnp.float32
ORB = 64
LANES = 128
SLABS = 12
LEVELS = (
    ((0, None, 1), (2, 1, 3), (4, 3, 5), (6, 5, 7), (8, 7, 9), (10, 9, 11)),
    ((1, None, 3), (5, 3, 7), (9, 7, 11)),
    ((3, None, 7), (11, 7, None)),
    ((7, None, None),),
)
STEPS = {6: 1, 3: 2, 2: 2, 1: 2}


def lane_of(shape):
    return lax.broadcasted_iota(jnp.int32, shape, len(shape) - 1)


def row_of(shape):
    return lax.broadcasted_iota(jnp.int32, shape, len(shape) - 2)


def times_i(value):
    turned = pltpu.roll(value, ORB, 1)
    return jnp.where(lane_of(value.shape) < ORB, -turned, turned)


def right_form(value):
    return jnp.concatenate([value, times_i(value)], axis=0)


def dot(left, right):
    return jnp.dot(left, right, precision=HIGHEST, preferred_element_type=F32)


def spread(row):
    return jnp.broadcast_to(row, (8, LANES))


def pack(values):
    first = lane_of((8, LANES)) < ORB
    pairs = []
    for at in range(0, len(values), 2):
        one = values[at]
        two = values[min(at + 1, len(values) - 1)]
        real, imag = [], []
        for t in range(0, ORB, 8):
            x, y = one[t : t + 8], two[t : t + 8]
            real.append(jnp.where(first, x, pltpu.roll(y, ORB, 1)))
            imag.append(jnp.where(first, pltpu.roll(x, ORB, 1), y))
        pairs.append((real, imag))
    return pairs


def unpack(pairs, count):
    first = lane_of((8, LANES)) < ORB
    values = []
    for real, imag in pairs:
        left = [jnp.where(first, r, pltpu.roll(i, ORB, 1)) for r, i in zip(real, imag)]
        values.append(jnp.concatenate(left, axis=0))
        if len(values) < count:
            right = [jnp.where(first, pltpu.roll(r, ORB, 1), i) for r, i in zip(real, imag)]
            values.append(jnp.concatenate(right, axis=0))
    return values


def pivot_inverse(gram, size):
    if size == 1:
        return [[(1.0 / gram[0, 0][0], None)]]
    one, two = gram[0, 0][0], gram[1, 1][0]
    re, im = gram[0, 1]
    scale = 1.0 / (one * two - re * re - im * im)
    re, im = re * scale, im * scale
    return [[(two * scale, None), (-re, -im)], [(-re, im), (one * scale, None)]]


def invert_all(values, size):
    lanes = lane_of((8, LANES))
    place = lanes & (ORB - 1)
    half = lanes & ORB
    rows = row_of((8, LANES))

    def column(tile, k):
        return jnp.take_along_axis(tile, half + k, axis=1, mode="promise_in_bounds")

    def pivot_block(real, imag, k):
        tile, row = divmod(k, 8)
        gram = {}
        for j in range(size):
            re, im = column(real[tile], k + j), column(imag[tile], k + j)
            for i in range(j + 1):
                at = slice(row + i, row + i + 1)
                gram[i, j] = (spread(re[at]), None if i == j else spread(im[at]))
        return gram

    state = [
        (real, imag, pivot_inverse(pivot_block(real, imag, 0), size))
        for real, imag in pack(values)
    ]
    for k in range(0, ORB, size):
        tile, row = divmod(k, 8)
        later = []
        for real, imag, small in state:
            cols = [
                ([column(x, k + j) for x in real], [column(x, k + j) for x in imag])
                for j in range(size)
            ]
            ahead = None
            if k + size < ORB:
                gram = pivot_block(real, imag, k + size)
                next_tile, next_row = divmod(k + size, 8)
                near = []
                for re, im in cols:
                    near.append([])
                    for i in range(size):
                        at = slice(next_row + i, next_row + i + 1)
                        near[-1].append((spread(re[next_tile][at]), spread(im[next_tile][at])))
                for j in range(size):
                    for m in range(size):
                        re = im = None
                        for q in range(size):
                            gr, gi = small[m][q]
                            cr, ci = near[q][j]
                            tr, ti = gr * cr, -(gr * ci)
                            if gi is not None:
                                tr, ti = tr + gi * ci, ti + gi * cr
                            re, im = (tr, ti) if re is None else (re + tr, im + ti)
                        for i in range(j + 1):
                            cr, ci = near[m][i]
                            old_re, old_im = gram[i, j]
                            new_re = old_re - (cr * re - ci * im)
                            new_im = None if i == j else old_im - (cr * im + ci * re)
                            gram[i, j] = (new_re, new_im)
                ahead = pivot_inverse(gram, size)
            tops = []
            for j in range(size):
                at = slice(row + j, row + j + 1)
                tops.append((spread(real[tile][at]), spread(imag[tile][at])))
            fresh = []
            for i in range(size):
                re = im = None
                for j in range(size):
                    gr, gi = small[i][j]
                    tr, ti = gr * tops[j][0], gr * tops[j][1]
                    if gi is not None:
                        tr, ti = tr - gi * tops[j][1], ti + gi * tops[j][0]
                    re, im = (tr, ti) if re is None else (re + tr, im + ti)
                for j in range(size):
                    gr, gi = small[i][j]
                    re = jnp.where(place == k + j, gr, re)
                    im = jnp.where(place == k + j, 0.0 if gi is None else gi, im)
                fresh.append((re, im))
            inside = (place >= k) & (place < k + size)
            new_real, new_imag = [], []
            for t in range(ORB // 8):
                re = jnp.where(inside, 0.0, real[t])
                im = jnp.where(inside, 0.0, imag[t])
                for j in range(size):
                    cr, ci = cols[j][0][t], cols[j][1][t]
                    re = re - cr * fresh[j][0] + ci * fresh[j][1]
                    im = im - cr * fresh[j][1] - ci * fresh[j][0]
                if t == tile:
                    for j in range(size):
                        re = jnp.where(rows == row + j, fresh[j][0], re)
                        im = jnp.where(rows == row + j, fresh[j][1], im)
                new_real.append(re)
                new_imag.append(im)
            later.append((new_real, new_imag, ahead))
        state = later
    return unpack([(real, imag) for real, imag, unused in state], len(values))


def link_slots():
    slots = {}
    for level in LEVELS:
        for s, l, r in level:
            near = [n for n in (l, r) if n is not None]
            for n in near:
                for m in near:
                    if m != n:
                        slots.setdefault((n, m), len(slots))
                slots.setdefault((s, n), len(slots))
                slots.setdefault((n, s), len(slots))
    return slots


SLOTS = link_slots()
INV, SOL, LINK = 0, SLABS, 2 * SLABS
KEPT = 2 * SLABS + len(SLOTS)


def climb(kept, rhs, sol):
    def link(i, j):
        return kept[LINK + SLOTS[i, j]]

    for level in reversed(LEVELS):
        for s, l, r in level:
            near = [n for n in (l, r) if n is not None]
            if not near:
                sol(s, rhs[s])
                continue
            steps = jnp.concatenate([link(s, n) for n in near], axis=1)
            values = jnp.concatenate([right_form(sol(n)) for n in near], axis=0)
            sol(s, rhs[s] - dot(steps, values))


def solve_kernel(in_ref, small_ref, kept, diag, rhs):
    def link(i, j):
        return LINK + SLOTS[i, j]

    corner = lane_of((ORB, LANES)) == row_of((ORB, LANES))
    for s in range(SLABS):
        group, i = divmod(s, 3)
        p = in_ref[group, 0, i * ORB : (i + 1) * ORB, :]
        q = in_ref[group, 1, i * ORB : (i + 1) * ORB, :]
        left = jnp.concatenate([p, q], axis=0)
        right = jnp.concatenate([p, times_i(p), q, times_i(q)], axis=0)
        both = lax.dot_general(
            left, right, (((1,), (1,)), ((), ())), precision=HIGHEST, preferred_element_type=F32
        )
        own = both[ORB:, LANES:]
        before = both[:ORB, :LANES]
        shift = jnp.broadcast_to(small_ref[group, i : i + 1, :], (ORB, LANES))
        own = own + jnp.where(corner, shift, 0.0)
        if s == 0:
            diag[s] = own + before
        else:
            diag[s] = own
            diag[s - 1] = diag[s - 1] + before
            kept[link(s - 1, s)] = -both[:ORB, LANES:]
            kept[link(s, s - 1)] = -both[ORB:, :LANES]
        for part in range(2):
            side, offset = divmod(i * ORB + part * 32, HALF_ROWS)
            rhs[s, part * 32 : part * 32 + 32, :] = in_ref[
                group, side, LINK_ROWS + offset : LINK_ROWS + offset + 32, :
            ]

    for level in LEVELS:
        inverses = invert_all([diag[s] for s, _, _ in level], STEPS[len(level)])
        for (s, l, r), inverse in zip(level, inverses):
            kept[INV + s] = inverse
        for s, l, r in level:
            near = [n for n in (l, r) if n is not None]
            sides = [right_form(kept[link(s, n)]) for n in near] + [right_form(rhs[s])]
            step = dot(kept[INV + s], jnp.concatenate(sides, axis=1))
            rhs[s] = step[:, LANES * len(near) :]
            if not near:
                continue
            back = jnp.concatenate([kept[link(n, s)] for n in near], axis=0)
            pieces = [step[:, LANES * i : LANES * (i + 1)] for i in range(len(near) + 1)]
            moved = dot(back, jnp.concatenate([right_form(piece) for piece in pieces], axis=1))
            for i, n in enumerate(near):
                kept[link(s, n)] = pieces[i]
                for j, m in enumerate(near):
                    block = moved[ORB * i : ORB * (i + 1), LANES * j : LANES * (j + 1)]
                    if n == m:
                        diag[n] = diag[n] - block
                    else:
                        kept[link(n, m)] = -block
                rhs[n] = rhs[n] - moved[ORB * i : ORB * (i + 1), LANES * len(near) :]

    def sol(s, value=None):
        if value is None:
            return kept[SOL + s]
        kept[SOL + s] = value

    climb(kept, rhs, sol)


def solve_retarded(gathered, small):
    return pl.pallas_call(
        solve_kernel,
        out_shape=jax.ShapeDtypeStruct((KEPT, ORB, LANES), F32),
        in_specs=[pl.BlockSpec(memory_space=pltpu.VMEM)] * 2,
        out_specs=pl.BlockSpec(memory_space=pltpu.VMEM),
        scratch_shapes=[
            pltpu.VMEM((SLABS, ORB, LANES), F32),
            pltpu.VMEM((SLABS, ORB, LANES), F32),
        ],
        compiler_params=pltpu.CompilerParams(vmem_limit_bytes=32 << 20),
        name="retarded",
    )(gathered, small)


ENERGIES = 64


def lag_kernel(in_ref, out_ref, gl, gg):
    first = lane_of((ENERGIES, LANES)) < ORB
    for half in range(2):
        gl[half, pl.ds(ENERGIES, 8), :] = jnp.zeros((8, LANES), F32)

    def one(index, unused):
        slab = index // 2
        orbital = index % 2
        sums = []
        for half in range(2):
            for parity in range(2):
                base = (half * 2 + parity) * (32 * 9) + slab * 3
                gl[half, pl.ds(parity, 32, stride=2), :] = in_ref[
                    pl.ds(base + orbital, 32, stride=9), :
                ]
                gg[half, pl.ds(parity, 32, stride=2), :] = in_ref[pl.ds(base + 2, 32, stride=9), :]
            power = gg[half]
            turned = pltpu.roll(power, ORB, 1)
            low = jnp.where(first, power, turned)
            high = jnp.where(first, turned, power)
            gg[half] = jnp.where(orbital == 0, low, high)
            acc = [jnp.zeros((8, LANES), F32) for _ in range(8)]
            for energy in range(ENERGIES):
                weight = jnp.broadcast_to(gg[half, energy : energy + 1, :], (8, LANES))
                for block in range((ENERGIES - energy + 7) // 8):
                    acc[block] = acc[block] + weight * gl[half, pl.ds(energy + 8 * block, 8), :]
            sums.append(jnp.concatenate(acc, axis=0))
        zero_turned = pltpu.roll(sums[0], ORB, 1)
        one_turned = pltpu.roll(sums[1], ORB, 1)
        scale = 1.0 / ENERGIES
        out_ref[pl.ds(index, ENERGIES, stride=6), :] = jnp.where(first, sums[0], one_turned) * scale
        out_ref[pl.ds(ENERGIES * 6 + index, ENERGIES, stride=6), :] = (
            jnp.where(first, zero_turned, sums[1]) * scale
        )
        return unused

    lax.fori_loop(0, 6, one, 0)


def correlate(received):
    return pl.pallas_call(
        lag_kernel,
        out_shape=jax.ShapeDtypeStruct((2 * ENERGIES * 6, LANES), F32),
        in_specs=[pl.BlockSpec(memory_space=pltpu.VMEM)],
        out_specs=pl.BlockSpec(memory_space=pltpu.VMEM),
        scratch_shapes=[
            pltpu.VMEM((2, ENERGIES + 8, LANES), F32),
            pltpu.VMEM((2, ENERGIES, LANES), F32),
        ],
        compiler_params=pltpu.CompilerParams(vmem_limit_bytes=32 << 20),
        name="lags",
    )(received)


GROUPS = 4
PER_GROUP = 32
LINK_ROWS = 3 * ORB
HALF_ROWS = LINK_ROWS // 2
PIECE_ROWS = LINK_ROWS + HALF_ROWS
CHUNKS = ((0, LINK_ROWS), (LINK_ROWS, HALF_ROWS))
MESH = pl.DeviceIdType.MESH


def gather_kernel(
    packed_ref, pair_ref, out_ref, small_ref,
    piece, small_piece, sent, arrived, passed, handed, small_sent, small_arrived,
):
    group = lax.axis_index("slab")
    spot = lax.axis_index("energy")
    core = lax.rem(spot, 2)
    sibling = spot + 1 - 2 * core
    barrier = pltpu.get_barrier_semaphore()
    for d in range(1, GROUPS):
        pl.semaphore_signal(
            barrier, inc=1, device_id=(lax.rem(group + d, GROUPS), spot), device_id_type=MESH
        )
    pl.semaphore_signal(barrier, inc=1, device_id=(group, sibling), device_id_type=MESH)
    my_half = group // 2

    first = lane_of((ORB, LANES)) < ORB
    for i in range(3):
        real, imag = packed_ref[i, 0, :, :LANES], packed_ref[i, 1, :, :LANES]
        p = jnp.where(first, real, pltpu.roll(imag, ORB, 1))
        q = jnp.where(first, pltpu.roll(real, ORB, 1), imag)
        span = pl.ds(i * ORB, ORB)
        out_ref[group, 0, span, :] = p
        out_ref[group, 1, span, :] = q
        mine = jnp.where(core == 0, p, q)
        piece[0, span, :] = mine
        piece[1, span, :] = mine
        real, imag = packed_ref[i, 0, :, LANES:], packed_ref[i, 1, :, LANES:]
        halves = (
            jnp.where(first, real, pltpu.roll(imag, ORB, 1)),
            jnp.where(first, pltpu.roll(real, ORB, 1), imag),
        )
        own = jnp.where(my_half == 0, halves[0], halves[1])
        for part in range(2):
            low = i * ORB + part * 32
            side, offset = divmod(low, HALF_ROWS)
            there = pl.ds(LINK_ROWS + offset, 32)
            rows = slice(part * 32, part * 32 + 32)
            out_ref[group, side, there, :] = own[rows]

            @pl.when(core == side)
            def _():
                piece[0, there, :] = halves[0][rows]
                piece[1, there, :] = halves[1][rows]

    pair = pair_ref[...]
    for parity in range(2):
        small_piece[parity, 0:3, :] = pair[:, parity]
    small_ref[group, 0:3, :] = jnp.where(lax.rem(group, 2) == 0, pair[:, 0], pair[:, 1])

    pl.semaphore_wait(barrier, GROUPS)
    copies = []
    smalls = []
    for d in (2, 1, 3):
        there = lax.rem(group + d, GROUPS)
        small = pltpu.make_async_remote_copy(
            src_ref=small_piece.at[lax.rem(there, 2)],
            dst_ref=small_ref.at[group],
            send_sem=small_sent.at[d],
            recv_sem=small_arrived.at[d],
            device_id=(there, spot),
            device_id_type=MESH,
        )
        small.start()
        smalls.append(small)
    for c, (low, rows) in enumerate(CHUNKS):
        for d in (2, 1, 3):
            there = lax.rem(group + d, GROUPS)
            copy = pltpu.make_async_remote_copy(
                src_ref=piece.at[there // 2, pl.ds(low, rows)],
                dst_ref=out_ref.at[group, core, pl.ds(low, rows)],
                send_sem=sent.at[c, d],
                recv_sem=arrived.at[c, d],
                device_id=(there, spot),
                device_id_type=MESH,
            )
            copy.start()
            copies.append((c, low, rows, d, copy))
    forwards = []
    for c, low, rows, d, copy in sorted(copies, key=lambda item: (item[0], (1, 3, 2).index(item[3]))):
        copy.wait_recv()
        source = lax.rem(group + GROUPS - d, GROUPS)
        forward = pltpu.make_async_remote_copy(
            src_ref=out_ref.at[source, core, pl.ds(low, rows)],
            dst_ref=out_ref.at[source, core, pl.ds(low, rows)],
            send_sem=passed.at[c, d],
            recv_sem=handed.at[c, d],
            device_id=(group, sibling),
            device_id_type=MESH,
        )
        forward.start()
        forwards.append(forward)
    for small in smalls:
        small.wait()
    for c, low, rows, d, copy in copies:
        copy.wait_send()
    for forward in forwards:
        forward.wait()


def gather_links(packed, pair):
    dma = pltpu.SemaphoreType.DMA
    return pl.pallas_call(
        gather_kernel,
        out_shape=(
            jax.ShapeDtypeStruct((GROUPS, 2, PIECE_ROWS, LANES), F32),
            jax.ShapeDtypeStruct((GROUPS, 8, LANES), F32),
        ),
        in_specs=[pl.BlockSpec(memory_space=pltpu.VMEM)] * 2,
        out_specs=[pl.BlockSpec(memory_space=pltpu.VMEM)] * 2,
        scratch_shapes=[
            pltpu.VMEM((2, PIECE_ROWS, LANES), F32),
            pltpu.VMEM((2, 8, LANES), F32),
            dma((2, GROUPS)),
            dma((2, GROUPS)),
            dma((2, GROUPS)),
            dma((2, GROUPS)),
            dma((GROUPS,)),
            dma((GROUPS,)),
        ],
        compiler_params=pltpu.CompilerParams(
            collective_id=0, has_side_effects=True, vmem_limit_bytes=16 << 20
        ),
        name="gather_links",
    )(packed, pair)


def exchange_kernel(kept, small_ref, out_ref, rhs, sol_ref, scratch, outgoing, sent, arrived, local):
    group = lax.axis_index("slab")
    spot = lax.axis_index("energy")
    here = group * PER_GROUP + spot
    count = GROUPS * PER_GROUP
    barrier = pltpu.get_barrier_semaphore()

    def greet(d, unused):
        there = lax.rem(here + d, count)
        pl.semaphore_signal(
            barrier,
            inc=1,
            device_id=(there // PER_GROUP, lax.rem(there, PER_GROUP)),
            device_id_type=MESH,
        )
        return unused

    lax.fori_loop(1, count, greet, 0)

    corner = lane_of((ORB, LANES)) == row_of((ORB, LANES)) + ORB
    for s in range(SLABS):
        row = jnp.broadcast_to(small_ref[s // 3, s % 3 : s % 3 + 1, :], (ORB, LANES))
        gain = jnp.sum(jnp.where(corner, row, 0.0), axis=1, keepdims=True)
        rhs[s] = gain * kept[SOL + s]
    for level in LEVELS:
        for s, l, r in level:
            near = [n for n in (l, r) if n is not None]
            step = dot(kept[INV + s], right_form(rhs[s]))
            rhs[s] = step
            if not near:
                continue
            back = jnp.concatenate([kept[LINK + SLOTS[n, s]] for n in near], axis=0)
            moved = dot(back, right_form(step))
            for i, n in enumerate(near):
                rhs[n] = rhs[n] - moved[ORB * i : ORB * (i + 1)]

    def sol(s, value=None):
        if value is None:
            return sol_ref[s]
        sol_ref[s] = value

    climb(kept, rhs, sol)
    first = lane_of((ORB, LANES)) < ORB
    for s in range(SLABS):
        x, y = kept[SOL + s], sol_ref[s]
        same = x * y
        crossed = pltpu.roll(x, ORB, 1) * y
        turned = x * pltpu.roll(y, ORB, 1)
        square = x * x
        scratch[0, s] = jnp.where(first, same + pltpu.roll(same, ORB, 1), crossed - turned)
        scratch[1, s] = square + pltpu.roll(square, ORB, 1)
        there = pl.ds((s // 3) * PER_GROUP, PER_GROUP)
        low = (s % 3) * 3
        even = scratch[1, s, pl.ds(0, 32, stride=2), :]
        odd = scratch[1, s, pl.ds(1, 32, stride=2), :]
        outgoing[there, low, 0, :] = scratch[0, s, pl.ds(0, 32, stride=2), :]
        outgoing[there, low + 1, 0, :] = scratch[0, s, pl.ds(1, 32, stride=2), :]
        outgoing[there, low + 2, 0, :] = jnp.where(lane_of((32, LANES)) < ORB, even, odd)

    own = pltpu.make_async_copy(outgoing.at[here], out_ref.at[here], local)
    own.start()
    pl.semaphore_wait(barrier, count - 1)

    def send(d, unused):
        there = lax.rem(here + d, count)
        pltpu.make_async_remote_copy(
            src_ref=outgoing.at[there],
            dst_ref=out_ref.at[here],
            send_sem=sent,
            recv_sem=arrived,
            device_id=(there // PER_GROUP, lax.rem(there, PER_GROUP)),
            device_id_type=MESH,
        ).start()
        return unused

    lax.fori_loop(1, count, send, 0)
    own.wait()
    others = pl.ds(0, count - 1)
    pltpu.make_async_copy(outgoing.at[others], outgoing.at[others], sent).wait()
    pltpu.make_async_copy(out_ref.at[others], out_ref.at[others], arrived).wait()


def lesser_and_exchange(kept, small):
    block = (GROUPS * PER_GROUP, 9, 1, LANES)
    return pl.pallas_call(
        exchange_kernel,
        out_shape=jax.ShapeDtypeStruct(block, F32),
        in_specs=[pl.BlockSpec(memory_space=pltpu.VMEM)] * 2,
        out_specs=pl.BlockSpec(memory_space=pltpu.VMEM),
        scratch_shapes=[
            pltpu.VMEM((SLABS, ORB, LANES), F32),
            pltpu.VMEM((SLABS, ORB, LANES), F32),
            pltpu.VMEM((2, SLABS, ORB, LANES), F32),
            pltpu.VMEM(block, F32),
            pltpu.SemaphoreType.DMA,
            pltpu.SemaphoreType.DMA,
            pltpu.SemaphoreType.DMA,
        ],
        compiler_params=pltpu.CompilerParams(
            collective_id=1, has_side_effects=True, vmem_limit_bytes=24 << 20
        ),
        name="lesser_and_exchange",
    )(kept, small)


def per_device(link_p, link_q, shift, lesser_gain, sources):
    packed = jnp.concatenate([link_p, link_q, sources], axis=-1)
    pair = jnp.swapaxes(jnp.concatenate([shift, lesser_gain], axis=-1), 0, 1)
    gathered, small = gather_links(packed, pair)
    kept = solve_retarded(gathered, small)
    received = lesser_and_exchange(kept, small)
    out = correlate(received.reshape(SLABS * 96, LANES))
    return out.reshape(2, ENERGIES, 3, 2, LANES)


def solution(mesh):
    placed = (
        P("slab", None, None, None),
        P("slab", None, None, None),
        P("energy", "slab", None),
        P("energy", "slab", None),
        P("slab", None, None, None),
    )
    return jax.shard_map(
        per_device,
        mesh=mesh,
        in_specs=placed,
        out_specs=P(None, None, "slab", "energy", None),
        check_vma=False,
    )
```

```python
import functools

import jax
import jax.numpy as jnp
from jax import lax
from jax.experimental import pallas as pl
from jax.experimental.pallas import tpu as pltpu
from jax.sharding import PartitionSpec as P

HIGHEST = lax.Precision.HIGHEST
F32 = jnp.float32
ORB = 64
LANES = 128
SLABS = 12
LEVELS = (
    ((0, None, 1), (2, 1, 3), (4, 3, 5), (6, 5, 7), (8, 7, 9), (10, 9, 11)),
    ((1, None, 3), (5, 3, 7), (9, 7, 11)),
    ((3, None, 7), (11, 7, None)),
    ((7, None, None),),
)
STEPS = {6: 1, 3: 2, 2: 2, 1: 2}


def lane_of(shape):
    return lax.broadcasted_iota(jnp.int32, shape, len(shape) - 1)


def row_of(shape):
    return lax.broadcasted_iota(jnp.int32, shape, len(shape) - 2)


def times_i(value):
    turned = pltpu.roll(value, ORB, 1)
    return jnp.where(lane_of(value.shape) < ORB, -turned, turned)


def right_form(value):
    return jnp.concatenate([value, times_i(value)], axis=0)


def dot(left, right):
    return jnp.dot(left, right, precision=HIGHEST, preferred_element_type=F32)


def spread(row):
    return jnp.broadcast_to(row, (8, LANES))


def pack(values):
    first = lane_of((8, LANES)) < ORB
    pairs = []
    for at in range(0, len(values), 2):
        one = values[at]
        two = values[min(at + 1, len(values) - 1)]
        real, imag = [], []
        for t in range(0, ORB, 8):
            x, y = one[t : t + 8], two[t : t + 8]
            real.append(jnp.where(first, x, pltpu.roll(y, ORB, 1)))
            imag.append(jnp.where(first, pltpu.roll(x, ORB, 1), y))
        pairs.append((real, imag))
    return pairs


def unpack(pairs, count):
    first = lane_of((8, LANES)) < ORB
    values = []
    for real, imag in pairs:
        left = [jnp.where(first, r, pltpu.roll(i, ORB, 1)) for r, i in zip(real, imag)]
        values.append(jnp.concatenate(left, axis=0))
        if len(values) < count:
            right = [jnp.where(first, pltpu.roll(r, ORB, 1), i) for r, i in zip(real, imag)]
            values.append(jnp.concatenate(right, axis=0))
    return values


def pivot_inverse(gram, size):
    if size == 1:
        return [[(1.0 / gram[0, 0][0], None)]]
    one, two = gram[0, 0][0], gram[1, 1][0]
    re, im = gram[0, 1]
    scale = 1.0 / (one * two - re * re - im * im)
    re, im = re * scale, im * scale
    return [[(two * scale, None), (-re, -im)], [(-re, im), (one * scale, None)]]


def invert_all(values, size):
    lanes = lane_of((8, LANES))
    place = lanes & (ORB - 1)
    half = lanes & ORB
    rows = row_of((8, LANES))

    def column(tile, k):
        return jnp.take_along_axis(tile, half + k, axis=1, mode="promise_in_bounds")

    def pivot_block(real, imag, k):
        tile, row = divmod(k, 8)
        gram = {}
        for j in range(size):
            re, im = column(real[tile], k + j), column(imag[tile], k + j)
            for i in range(j + 1):
                at = slice(row + i, row + i + 1)
                gram[i, j] = (spread(re[at]), None if i == j else spread(im[at]))
        return gram

    state = [
        (real, imag, pivot_inverse(pivot_block(real, imag, 0), size))
        for real, imag in pack(values)
    ]
    for k in range(0, ORB, size):
        tile, row = divmod(k, 8)
        later = []
        for real, imag, small in state:
            cols = [
                ([column(x, k + j) for x in real], [column(x, k + j) for x in imag])
                for j in range(size)
            ]
            ahead = None
            if k + size < ORB:
                gram = pivot_block(real, imag, k + size)
                next_tile, next_row = divmod(k + size, 8)
                near = []
                for re, im in cols:
                    near.append([])
                    for i in range(size):
                        at = slice(next_row + i, next_row + i + 1)
                        near[-1].append((spread(re[next_tile][at]), spread(im[next_tile][at])))
                for j in range(size):
                    for m in range(size):
                        re = im = None
                        for q in range(size):
                            gr, gi = small[m][q]
                            cr, ci = near[q][j]
                            tr, ti = gr * cr, -(gr * ci)
                            if gi is not None:
                                tr, ti = tr + gi * ci, ti + gi * cr
                            re, im = (tr, ti) if re is None else (re + tr, im + ti)
                        for i in range(j + 1):
                            cr, ci = near[m][i]
                            old_re, old_im = gram[i, j]
                            new_re = old_re - (cr * re - ci * im)
                            new_im = None if i == j else old_im - (cr * im + ci * re)
                            gram[i, j] = (new_re, new_im)
                ahead = pivot_inverse(gram, size)
            tops = []
            for j in range(size):
                at = slice(row + j, row + j + 1)
                tops.append((spread(real[tile][at]), spread(imag[tile][at])))
            fresh = []
            for i in range(size):
                re = im = None
                for j in range(size):
                    gr, gi = small[i][j]
                    tr, ti = gr * tops[j][0], gr * tops[j][1]
                    if gi is not None:
                        tr, ti = tr - gi * tops[j][1], ti + gi * tops[j][0]
                    re, im = (tr, ti) if re is None else (re + tr, im + ti)
                for j in range(size):
                    gr, gi = small[i][j]
                    re = jnp.where(place == k + j, gr, re)
                    im = jnp.where(place == k + j, 0.0 if gi is None else gi, im)
                fresh.append((re, im))
            inside = (place >= k) & (place < k + size)
            new_real, new_imag = [], []
            for t in range(ORB // 8):
                re = jnp.where(inside, 0.0, real[t])
                im = jnp.where(inside, 0.0, imag[t])
                for j in range(size):
                    cr, ci = cols[j][0][t], cols[j][1][t]
                    re = re - cr * fresh[j][0] + ci * fresh[j][1]
                    im = im - cr * fresh[j][1] - ci * fresh[j][0]
                if t == tile:
                    for j in range(size):
                        re = jnp.where(rows == row + j, fresh[j][0], re)
                        im = jnp.where(rows == row + j, fresh[j][1], im)
                new_real.append(re)
                new_imag.append(im)
            later.append((new_real, new_imag, ahead))
        state = later
    return unpack([(real, imag) for real, imag, unused in state], len(values))


def link_slots():
    slots = {}
    for level in LEVELS:
        for s, l, r in level:
            near = [n for n in (l, r) if n is not None]
            for n in near:
                for m in near:
                    if m != n:
                        slots.setdefault((n, m), len(slots))
                slots.setdefault((s, n), len(slots))
                slots.setdefault((n, s), len(slots))
    return slots


SLOTS = link_slots()
INV, SOL, LINK = 0, SLABS, 2 * SLABS
KEPT = 2 * SLABS + len(SLOTS)


def climb(kept, rhs, sol):
    def link(i, j):
        return kept[LINK + SLOTS[i, j]]

    for level in reversed(LEVELS):
        for s, l, r in level:
            near = [n for n in (l, r) if n is not None]
            if not near:
                sol(s, rhs[s])
                continue
            steps = jnp.concatenate([link(s, n) for n in near], axis=1)
            values = jnp.concatenate([right_form(sol(n)) for n in near], axis=0)
            sol(s, rhs[s] - dot(steps, values))


def solve_kernel(in_ref, small_ref, kept, diag, rhs):
    def link(i, j):
        return LINK + SLOTS[i, j]

    corner = lane_of((ORB, LANES)) == row_of((ORB, LANES))
    for s in range(SLABS):
        group, i = divmod(s, 3)
        p = in_ref[group, 0, i * ORB : (i + 1) * ORB, :]
        q = in_ref[group, 1, i * ORB : (i + 1) * ORB, :]
        left = jnp.concatenate([p, q], axis=0)
        right = jnp.concatenate([p, times_i(p), q, times_i(q)], axis=0)
        both = lax.dot_general(
            left, right, (((1,), (1,)), ((), ())), precision=HIGHEST, preferred_element_type=F32
        )
        own = both[ORB:, LANES:]
        before = both[:ORB, :LANES]
        shift = jnp.broadcast_to(small_ref[group, i : i + 1, :], (ORB, LANES))
        own = own + jnp.where(corner, shift, 0.0)
        if s == 0:
            diag[s] = own + before
        else:
            diag[s] = own
            diag[s - 1] = diag[s - 1] + before
            kept[link(s - 1, s)] = -both[:ORB, LANES:]
            kept[link(s, s - 1)] = -both[ORB:, :LANES]
        for part in range(2):
            side, offset = divmod(i * ORB + part * 32, HALF_ROWS)
            rhs[s, part * 32 : part * 32 + 32, :] = in_ref[
                group, side, LINK_ROWS + offset : LINK_ROWS + offset + 32, :
            ]

    for level in LEVELS:
        inverses = invert_all([diag[s] for s, _, _ in level], STEPS[len(level)])
        for (s, l, r), inverse in zip(level, inverses):
            kept[INV + s] = inverse
        for s, l, r in level:
            near = [n for n in (l, r) if n is not None]
            sides = [right_form(kept[link(s, n)]) for n in near] + [right_form(rhs[s])]
            step = dot(kept[INV + s], jnp.concatenate(sides, axis=1))
            rhs[s] = step[:, LANES * len(near) :]
            if not near:
                continue
            back = jnp.concatenate([kept[link(n, s)] for n in near], axis=0)
            pieces = [step[:, LANES * i : LANES * (i + 1)] for i in range(len(near) + 1)]
            moved = dot(back, jnp.concatenate([right_form(piece) for piece in pieces], axis=1))
            for i, n in enumerate(near):
                kept[link(s, n)] = pieces[i]
                for j, m in enumerate(near):
                    block = moved[ORB * i : ORB * (i + 1), LANES * j : LANES * (j + 1)]
                    if n == m:
                        diag[n] = diag[n] - block
                    else:
                        kept[link(n, m)] = -block
                rhs[n] = rhs[n] - moved[ORB * i : ORB * (i + 1), LANES * len(near) :]

    def sol(s, value=None):
        if value is None:
            return kept[SOL + s]
        kept[SOL + s] = value

    climb(kept, rhs, sol)


def solve_retarded(gathered, small):
    return pl.pallas_call(
        solve_kernel,
        out_shape=jax.ShapeDtypeStruct((KEPT, ORB, LANES), F32),
        in_specs=[pl.BlockSpec(memory_space=pltpu.VMEM)] * 2,
        out_specs=pl.BlockSpec(memory_space=pltpu.VMEM),
        scratch_shapes=[
            pltpu.VMEM((SLABS, ORB, LANES), F32),
            pltpu.VMEM((SLABS, ORB, LANES), F32),
        ],
        compiler_params=pltpu.CompilerParams(vmem_limit_bytes=32 << 20),
        name="retarded",
    )(gathered, small)


ENERGIES = 64


def lag_kernel(in_ref, out_ref, gl, gg):
    first = lane_of((ENERGIES, LANES)) < ORB
    for half in range(2):
        gl[half, pl.ds(ENERGIES, 8), :] = jnp.zeros((8, LANES), F32)

    def one(index, unused):
        slab = index // 2
        orbital = index % 2
        sums = []
        for half in range(2):
            for parity in range(2):
                base = (half * 2 + parity) * (32 * 9) + slab * 3
                gl[half, pl.ds(parity, 32, stride=2), :] = in_ref[
                    pl.ds(base + orbital, 32, stride=9), :
                ]
                gg[half, pl.ds(parity, 32, stride=2), :] = in_ref[pl.ds(base + 2, 32, stride=9), :]
            power = gg[half]
            turned = pltpu.roll(power, ORB, 1)
            low = jnp.where(first, power, turned)
            high = jnp.where(first, turned, power)
            gg[half] = jnp.where(orbital == 0, low, high)
            acc = [jnp.zeros((8, LANES), F32) for _ in range(8)]
            for energy in range(ENERGIES):
                weight = jnp.broadcast_to(gg[half, energy : energy + 1, :], (8, LANES))
                for block in range((ENERGIES - energy + 7) // 8):
                    acc[block] = acc[block] + weight * gl[half, pl.ds(energy + 8 * block, 8), :]
            sums.append(jnp.concatenate(acc, axis=0))
        zero_turned = pltpu.roll(sums[0], ORB, 1)
        one_turned = pltpu.roll(sums[1], ORB, 1)
        scale = 1.0 / ENERGIES
        out_ref[pl.ds(index, ENERGIES, stride=6), :] = jnp.where(first, sums[0], one_turned) * scale
        out_ref[pl.ds(ENERGIES * 6 + index, ENERGIES, stride=6), :] = (
            jnp.where(first, zero_turned, sums[1]) * scale
        )
        return unused

    lax.fori_loop(0, 6, one, 0)


def correlate(received):
    return pl.pallas_call(
        lag_kernel,
        out_shape=jax.ShapeDtypeStruct((2 * ENERGIES * 6, LANES), F32),
        in_specs=[pl.BlockSpec(memory_space=pltpu.VMEM)],
        out_specs=pl.BlockSpec(memory_space=pltpu.VMEM),
        scratch_shapes=[
            pltpu.VMEM((2, ENERGIES + 8, LANES), F32),
            pltpu.VMEM((2, ENERGIES, LANES), F32),
        ],
        compiler_params=pltpu.CompilerParams(vmem_limit_bytes=32 << 20),
        name="lags",
    )(received)


GROUPS = 4
PER_GROUP = 32
LINK_ROWS = 3 * ORB
HALF_ROWS = LINK_ROWS // 2
PIECE_ROWS = LINK_ROWS + HALF_ROWS
MESH = pl.DeviceIdType.MESH


def gather_kernel(
    packed_ref, pair_ref, out_ref, small_ref,
    piece, small_piece, sent, arrived, passed, handed, small_sent, small_arrived,
):
    group = lax.axis_index("slab")
    spot = lax.axis_index("energy")
    core = lax.rem(spot, 2)
    sibling = spot + 1 - 2 * core
    barrier = pltpu.get_barrier_semaphore()
    for d in range(1, GROUPS):
        pl.semaphore_signal(
            barrier, inc=1, device_id=(lax.rem(group + d, GROUPS), spot), device_id_type=MESH
        )
    pl.semaphore_signal(barrier, inc=1, device_id=(group, sibling), device_id_type=MESH)
    my_half = group // 2

    first = lane_of((ORB, LANES)) < ORB
    for i in range(3):
        real, imag = packed_ref[i, 0, :, :LANES], packed_ref[i, 1, :, :LANES]
        p = jnp.where(first, real, pltpu.roll(imag, ORB, 1))
        q = jnp.where(first, pltpu.roll(real, ORB, 1), imag)
        span = pl.ds(i * ORB, ORB)
        out_ref[group, 0, span, :] = p
        out_ref[group, 1, span, :] = q
        mine = jnp.where(core == 0, p, q)
        piece[0, span, :] = mine
        piece[1, span, :] = mine
        real, imag = packed_ref[i, 0, :, LANES:], packed_ref[i, 1, :, LANES:]
        halves = (
            jnp.where(first, real, pltpu.roll(imag, ORB, 1)),
            jnp.where(first, pltpu.roll(real, ORB, 1), imag),
        )
        own = jnp.where(my_half == 0, halves[0], halves[1])
        for part in range(2):
            low = i * ORB + part * 32
            side, offset = divmod(low, HALF_ROWS)
            there = pl.ds(LINK_ROWS + offset, 32)
            rows = slice(part * 32, part * 32 + 32)
            out_ref[group, side, there, :] = own[rows]

            @pl.when(core == side)
            def _():
                piece[0, there, :] = halves[0][rows]
                piece[1, there, :] = halves[1][rows]

    pair = pair_ref[...]
    for parity in range(2):
        small_piece[parity, 0:3, :] = pair[:, parity]
    small_ref[group, 0:3, :] = jnp.where(lax.rem(group, 2) == 0, pair[:, 0], pair[:, 1])

    pl.semaphore_wait(barrier, GROUPS)
    smalls = []
    for d in (2, 1, 3):
        there = lax.rem(group + d, GROUPS)
        small = pltpu.make_async_remote_copy(
            src_ref=small_piece.at[lax.rem(there, 2)],
            dst_ref=small_ref.at[group],
            send_sem=small_sent.at[d],
            recv_sem=small_arrived.at[d],
            device_id=(there, spot),
            device_id_type=MESH,
        )
        small.start()
        smalls.append(small)
    def rows_at(chunk):
        return pl.ds(chunk * HALF_ROWS, HALF_ROWS)

    def to_group(chunk, d, there, source_ref, origin):
        return pltpu.make_async_remote_copy(
            src_ref=source_ref,
            dst_ref=out_ref.at[origin, core, rows_at(chunk)],
            send_sem=sent.at[chunk, d],
            recv_sem=arrived.at[chunk, d],
            device_id=(there, spot),
            device_id_type=MESH,
        )

    copies = {}
    for chunk, d in ((0, 1), (1, 3), (1, 1), (0, 3), (2, 2), (2, 1), (2, 3)):
        there = lax.rem(group + d, GROUPS)
        half = there // 2 if chunk == 2 else 0
        copies[chunk, d] = to_group(chunk, d, there, piece.at[half, rows_at(chunk)], group)
        copies[chunk, d].start()
    forwards = []
    for chunk, d in ((0, 1), (1, 3), (1, 1), (0, 3), (2, 1), (2, 3), (0, 2), (1, 2), (2, 2)):
        origin = lax.rem(group + GROUPS - d, GROUPS)
        copies[chunk, d].wait_recv()
        here = out_ref.at[origin, core, rows_at(chunk)]
        if (chunk, d) in ((0, 1), (1, 3)):
            copies[chunk, 2] = to_group(chunk, 2, lax.rem(group + d, GROUPS), here, origin)
            copies[chunk, 2].start()
        forward = pltpu.make_async_remote_copy(
            src_ref=here,
            dst_ref=here,
            send_sem=passed.at[chunk, d],
            recv_sem=handed.at[chunk, d],
            device_id=(group, sibling),
            device_id_type=MESH,
        )
        forward.start()
        forwards.append(forward)
    for small in smalls:
        small.wait()
    for copy in copies.values():
        copy.wait_send()
    for forward in forwards:
        forward.wait()


def gather_links(packed, pair):
    dma = pltpu.SemaphoreType.DMA
    return pl.pallas_call(
        gather_kernel,
        out_shape=(
            jax.ShapeDtypeStruct((GROUPS, 2, PIECE_ROWS, LANES), F32),
            jax.ShapeDtypeStruct((GROUPS, 8, LANES), F32),
        ),
        in_specs=[pl.BlockSpec(memory_space=pltpu.VMEM)] * 2,
        out_specs=[pl.BlockSpec(memory_space=pltpu.VMEM)] * 2,
        scratch_shapes=[
            pltpu.VMEM((2, PIECE_ROWS, LANES), F32),
            pltpu.VMEM((2, 8, LANES), F32),
            dma((3, GROUPS)),
            dma((3, GROUPS)),
            dma((3, GROUPS)),
            dma((3, GROUPS)),
            dma((GROUPS,)),
            dma((GROUPS,)),
        ],
        compiler_params=pltpu.CompilerParams(
            collective_id=0, has_side_effects=True, vmem_limit_bytes=16 << 20
        ),
        name="gather_links",
    )(packed, pair)


def exchange_kernel(kept, small_ref, out_ref, rhs, sol_ref, scratch, outgoing, sent, arrived, local):
    group = lax.axis_index("slab")
    spot = lax.axis_index("energy")
    here = group * PER_GROUP + spot
    count = GROUPS * PER_GROUP
    barrier = pltpu.get_barrier_semaphore()

    def greet(d, unused):
        there = lax.rem(here + d, count)
        pl.semaphore_signal(
            barrier,
            inc=1,
            device_id=(there // PER_GROUP, lax.rem(there, PER_GROUP)),
            device_id_type=MESH,
        )
        return unused

    def greet_eight(i, unused):
        for j in range(8):
            greet(1 + 8 * i + j, 0)
        return unused

    full = (count - 1) // 8
    lax.fori_loop(0, full, greet_eight, 0)
    for d in range(1 + 8 * full, count):
        greet(d, 0)

    corner = lane_of((ORB, LANES)) == row_of((ORB, LANES)) + ORB
    for s in range(SLABS):
        row = jnp.broadcast_to(small_ref[s // 3, s % 3 : s % 3 + 1, :], (ORB, LANES))
        gain = jnp.sum(jnp.where(corner, row, 0.0), axis=1, keepdims=True)
        rhs[s] = gain * kept[SOL + s]
    for level in LEVELS:
        for s, l, r in level:
            near = [n for n in (l, r) if n is not None]
            step = dot(kept[INV + s], right_form(rhs[s]))
            rhs[s] = step
            if not near:
                continue
            back = jnp.concatenate([kept[LINK + SLOTS[n, s]] for n in near], axis=0)
            moved = dot(back, right_form(step))
            for i, n in enumerate(near):
                rhs[n] = rhs[n] - moved[ORB * i : ORB * (i + 1)]

    def sol(s, value=None):
        if value is None:
            return sol_ref[s]
        sol_ref[s] = value

    climb(kept, rhs, sol)
    first = lane_of((ORB, LANES)) < ORB
    for s in range(SLABS):
        x, y = kept[SOL + s], sol_ref[s]
        same = x * y
        crossed = pltpu.roll(x, ORB, 1) * y
        turned = x * pltpu.roll(y, ORB, 1)
        square = x * x
        scratch[0, s] = jnp.where(first, same + pltpu.roll(same, ORB, 1), crossed - turned)
        scratch[1, s] = square + pltpu.roll(square, ORB, 1)
        there = pl.ds((s // 3) * PER_GROUP, PER_GROUP)
        low = (s % 3) * 3
        even = scratch[1, s, pl.ds(0, 32, stride=2), :]
        odd = scratch[1, s, pl.ds(1, 32, stride=2), :]
        outgoing[there, low, 0, :] = scratch[0, s, pl.ds(0, 32, stride=2), :]
        outgoing[there, low + 1, 0, :] = scratch[0, s, pl.ds(1, 32, stride=2), :]
        outgoing[there, low + 2, 0, :] = jnp.where(lane_of((32, LANES)) < ORB, even, odd)

    own = pltpu.make_async_copy(outgoing.at[here], out_ref.at[here], local)
    own.start()
    pl.semaphore_wait(barrier, count - 1)

    def send(there):
        pltpu.make_async_remote_copy(
            src_ref=outgoing.at[there],
            dst_ref=out_ref.at[here],
            send_sem=sent,
            recv_sem=arrived,
            device_id=(there // PER_GROUP, lax.rem(there, PER_GROUP)),
            device_id_type=MESH,
        ).start()

    z, x, core = spot // 8, lax.rem(spot // 2, 4), lax.rem(spot, 2)
    hops = (0, 1, 2, 1)
    planes = [(dy, dz) for dy in range(4) for dz in range(4)]
    planes.sort(key=lambda plane: -(hops[plane[0]] + hops[plane[1]]))
    for dy, dz in planes:
        plane = lax.rem(group + dy, 4) * PER_GROUP + lax.rem(z + dz, 4) * 8

        def spread_x(i, unused):
            dx = lax.rem(i // 2 + 2, 4)
            send(plane + lax.rem(x + dx, 4) * 2 + lax.rem(core + i, 2))
            return unused

        if (dy, dz) == (0, 0):
            for i in (0, 1, 2, 3, 6, 7, 5):
                spread_x(jnp.int32(i), 0)
        else:
            lax.fori_loop(0, 8, spread_x, 0, unroll=True)
    own.wait()
    others = pl.ds(0, count - 1)
    pltpu.make_async_copy(outgoing.at[others], outgoing.at[others], sent).wait()
    pltpu.make_async_copy(out_ref.at[others], out_ref.at[others], arrived).wait()


def lesser_and_exchange(kept, small):
    block = (GROUPS * PER_GROUP, 9, 1, LANES)
    return pl.pallas_call(
        exchange_kernel,
        out_shape=jax.ShapeDtypeStruct(block, F32),
        in_specs=[pl.BlockSpec(memory_space=pltpu.VMEM)] * 2,
        out_specs=pl.BlockSpec(memory_space=pltpu.VMEM),
        scratch_shapes=[
            pltpu.VMEM((SLABS, ORB, LANES), F32),
            pltpu.VMEM((SLABS, ORB, LANES), F32),
            pltpu.VMEM((2, SLABS, ORB, LANES), F32),
            pltpu.VMEM(block, F32),
            pltpu.SemaphoreType.DMA,
            pltpu.SemaphoreType.DMA,
            pltpu.SemaphoreType.DMA,
        ],
        compiler_params=pltpu.CompilerParams(
            collective_id=1, has_side_effects=True, vmem_limit_bytes=24 << 20
        ),
        name="lesser_and_exchange",
    )(kept, small)


def per_device(link_p, link_q, shift, lesser_gain, sources):
    packed = jnp.concatenate([link_p, link_q, sources], axis=-1)
    pair = jnp.swapaxes(jnp.concatenate([shift, lesser_gain], axis=-1), 0, 1)
    gathered, small = gather_links(packed, pair)
    kept = solve_retarded(gathered, small)
    received = lesser_and_exchange(kept, small)
    out = correlate(received.reshape(SLABS * 96, LANES))
    return out.reshape(2, ENERGIES, 3, 2, LANES)


def solution(mesh):
    placed = (
        P("slab", None, None, None),
        P("slab", None, None, None),
        P("energy", "slab", None),
        P("energy", "slab", None),
        P("slab", None, None, None),
    )
    return jax.shard_map(
        per_device,
        mesh=mesh,
        in_specs=placed,
        out_specs=P(None, None, "slab", "energy", None),
        check_vma=False,
    )
```

```python
import functools

import jax
import jax.numpy as jnp
from jax import lax
from jax.experimental import pallas as pl
from jax.experimental.pallas import tpu as pltpu
from jax.sharding import PartitionSpec as P

HIGHEST = lax.Precision.HIGHEST
F32 = jnp.float32
ORB = 64
LANES = 128
SLABS = 12
LEVELS = (
    ((0, None, 1), (2, 1, 3), (4, 3, 5), (6, 5, 7), (8, 7, 9), (10, 9, 11)),
    ((1, None, 3), (5, 3, 7), (9, 7, 11)),
    ((3, None, 7), (11, 7, None)),
    ((7, None, None),),
)
STEPS = {6: 1, 3: 2, 2: 2, 1: 2}


def lane_of(shape):
    return lax.broadcasted_iota(jnp.int32, shape, len(shape) - 1)


def row_of(shape):
    return lax.broadcasted_iota(jnp.int32, shape, len(shape) - 2)


def times_i(value):
    turned = pltpu.roll(value, ORB, 1)
    return jnp.where(lane_of(value.shape) < ORB, -turned, turned)


def right_form(value):
    return jnp.concatenate([value, times_i(value)], axis=0)


def dot(left, right):
    return jnp.dot(left, right, precision=HIGHEST, preferred_element_type=F32)


def spread(row):
    return jnp.broadcast_to(row, (8, LANES))


def pack(values):
    first = lane_of((8, LANES)) < ORB
    pairs = []
    for at in range(0, len(values), 2):
        one = values[at]
        two = values[min(at + 1, len(values) - 1)]
        real, imag = [], []
        for t in range(0, ORB, 8):
            x, y = one[t : t + 8], two[t : t + 8]
            real.append(jnp.where(first, x, pltpu.roll(y, ORB, 1)))
            imag.append(jnp.where(first, pltpu.roll(x, ORB, 1), y))
        pairs.append((real, imag))
    return pairs


def unpack(pairs, count):
    first = lane_of((8, LANES)) < ORB
    values = []
    for real, imag in pairs:
        left = [jnp.where(first, r, pltpu.roll(i, ORB, 1)) for r, i in zip(real, imag)]
        values.append(jnp.concatenate(left, axis=0))
        if len(values) < count:
            right = [jnp.where(first, pltpu.roll(r, ORB, 1), i) for r, i in zip(real, imag)]
            values.append(jnp.concatenate(right, axis=0))
    return values


def pivot_inverse(gram, size):
    if size == 1:
        return [[(1.0 / gram[0, 0][0], None)]]
    one, two = gram[0, 0][0], gram[1, 1][0]
    re, im = gram[0, 1]
    scale = 1.0 / (one * two - re * re - im * im)
    re, im = re * scale, im * scale
    return [[(two * scale, None), (-re, -im)], [(-re, im), (one * scale, None)]]


def invert_all(values, size):
    lanes = lane_of((8, LANES))
    place = lanes & (ORB - 1)
    half = lanes & ORB
    rows = row_of((8, LANES))

    def column(tile, k):
        return jnp.take_along_axis(tile, half + k, axis=1, mode="promise_in_bounds")

    def pivot_block(real, imag, k):
        tile, row = divmod(k, 8)
        gram = {}
        for j in range(size):
            re, im = column(real[tile], k + j), column(imag[tile], k + j)
            for i in range(j + 1):
                at = slice(row + i, row + i + 1)
                gram[i, j] = (spread(re[at]), None if i == j else spread(im[at]))
        return gram

    state = [
        (real, imag, pivot_inverse(pivot_block(real, imag, 0), size))
        for real, imag in pack(values)
    ]
    for k in range(0, ORB, size):
        tile, row = divmod(k, 8)
        later = []
        for real, imag, small in state:
            cols = [
                ([column(x, k + j) for x in real], [column(x, k + j) for x in imag])
                for j in range(size)
            ]
            ahead = None
            if k + size < ORB:
                gram = pivot_block(real, imag, k + size)
                next_tile, next_row = divmod(k + size, 8)
                near = []
                for re, im in cols:
                    near.append([])
                    for i in range(size):
                        at = slice(next_row + i, next_row + i + 1)
                        near[-1].append((spread(re[next_tile][at]), spread(im[next_tile][at])))
                for j in range(size):
                    for m in range(size):
                        re = im = None
                        for q in range(size):
                            gr, gi = small[m][q]
                            cr, ci = near[q][j]
                            tr, ti = gr * cr, -(gr * ci)
                            if gi is not None:
                                tr, ti = tr + gi * ci, ti + gi * cr
                            re, im = (tr, ti) if re is None else (re + tr, im + ti)
                        for i in range(j + 1):
                            cr, ci = near[m][i]
                            old_re, old_im = gram[i, j]
                            new_re = old_re - (cr * re - ci * im)
                            new_im = None if i == j else old_im - (cr * im + ci * re)
                            gram[i, j] = (new_re, new_im)
                ahead = pivot_inverse(gram, size)
            tops = []
            for j in range(size):
                at = slice(row + j, row + j + 1)
                tops.append((spread(real[tile][at]), spread(imag[tile][at])))
            fresh = []
            for i in range(size):
                re = im = None
                for j in range(size):
                    gr, gi = small[i][j]
                    tr, ti = gr * tops[j][0], gr * tops[j][1]
                    if gi is not None:
                        tr, ti = tr - gi * tops[j][1], ti + gi * tops[j][0]
                    re, im = (tr, ti) if re is None else (re + tr, im + ti)
                for j in range(size):
                    gr, gi = small[i][j]
                    re = jnp.where(place == k + j, gr, re)
                    im = jnp.where(place == k + j, 0.0 if gi is None else gi, im)
                fresh.append((re, im))
            inside = (place >= k) & (place < k + size)
            new_real, new_imag = [], []
            for t in range(ORB // 8):
                re = jnp.where(inside, 0.0, real[t])
                im = jnp.where(inside, 0.0, imag[t])
                for j in range(size):
                    cr, ci = cols[j][0][t], cols[j][1][t]
                    re = re - cr * fresh[j][0] + ci * fresh[j][1]
                    im = im - cr * fresh[j][1] - ci * fresh[j][0]
                if t == tile:
                    for j in range(size):
                        re = jnp.where(rows == row + j, fresh[j][0], re)
                        im = jnp.where(rows == row + j, fresh[j][1], im)
                new_real.append(re)
                new_imag.append(im)
            later.append((new_real, new_imag, ahead))
        state = later
    return unpack([(real, imag) for real, imag, unused in state], len(values))


def link_slots():
    slots = {}
    for level in LEVELS:
        for s, l, r in level:
            near = [n for n in (l, r) if n is not None]
            for n in near:
                for m in near:
                    if m != n:
                        slots.setdefault((n, m), len(slots))
                slots.setdefault((s, n), len(slots))
                slots.setdefault((n, s), len(slots))
    return slots


SLOTS = link_slots()
INV, SOL, LINK = 0, SLABS, 2 * SLABS
KEPT = 2 * SLABS + len(SLOTS)


def climb(kept, rhs, sol):
    def link(i, j):
        return kept[LINK + SLOTS[i, j]]

    for level in reversed(LEVELS):
        for s, l, r in level:
            near = [n for n in (l, r) if n is not None]
            if not near:
                sol(s, rhs[s])
                continue
            steps = jnp.concatenate([link(s, n) for n in near], axis=1)
            values = jnp.concatenate([right_form(sol(n)) for n in near], axis=0)
            sol(s, rhs[s] - dot(steps, values))


def solve_kernel(in_ref, small_ref, kept, diag, rhs):
    def link(i, j):
        return LINK + SLOTS[i, j]

    corner = lane_of((ORB, LANES)) == row_of((ORB, LANES))
    for s in range(SLABS):
        group, i = divmod(s, 3)
        p = in_ref[group, 0, i * ORB : (i + 1) * ORB, :]
        q = in_ref[group, 1, i * ORB : (i + 1) * ORB, :]
        left = jnp.concatenate([p, q], axis=0)
        right = jnp.concatenate([p, times_i(p), q, times_i(q)], axis=0)
        both = lax.dot_general(
            left, right, (((1,), (1,)), ((), ())), precision=HIGHEST, preferred_element_type=F32
        )
        own = both[ORB:, LANES:]
        before = both[:ORB, :LANES]
        shift = jnp.broadcast_to(small_ref[group, i : i + 1, :], (ORB, LANES))
        own = own + jnp.where(corner, shift, 0.0)
        if s == 0:
            diag[s] = own + before
        else:
            diag[s] = own
            diag[s - 1] = diag[s - 1] + before
            kept[link(s - 1, s)] = -both[:ORB, LANES:]
            kept[link(s, s - 1)] = -both[ORB:, :LANES]
        for part in range(2):
            side, offset = divmod(i * ORB + part * 32, HALF_ROWS)
            rhs[s, part * 32 : part * 32 + 32, :] = in_ref[
                group, side, LINK_ROWS + offset : LINK_ROWS + offset + 32, :
            ]

    for level in LEVELS:
        inverses = invert_all([diag[s] for s, _, _ in level], STEPS[len(level)])
        for (s, l, r), inverse in zip(level, inverses):
            kept[INV + s] = inverse
        for s, l, r in level:
            near = [n for n in (l, r) if n is not None]
            sides = [right_form(kept[link(s, n)]) for n in near] + [right_form(rhs[s])]
            step = dot(kept[INV + s], jnp.concatenate(sides, axis=1))
            rhs[s] = step[:, LANES * len(near) :]
            if not near:
                continue
            back = jnp.concatenate([kept[link(n, s)] for n in near], axis=0)
            pieces = [step[:, LANES * i : LANES * (i + 1)] for i in range(len(near) + 1)]
            moved = dot(back, jnp.concatenate([right_form(piece) for piece in pieces], axis=1))
            for i, n in enumerate(near):
                kept[link(s, n)] = pieces[i]
                for j, m in enumerate(near):
                    block = moved[ORB * i : ORB * (i + 1), LANES * j : LANES * (j + 1)]
                    if n == m:
                        diag[n] = diag[n] - block
                    else:
                        kept[link(n, m)] = -block
                rhs[n] = rhs[n] - moved[ORB * i : ORB * (i + 1), LANES * len(near) :]

    def sol(s, value=None):
        if value is None:
            return kept[SOL + s]
        kept[SOL + s] = value

    climb(kept, rhs, sol)


def solve_retarded(gathered, small):
    return pl.pallas_call(
        solve_kernel,
        out_shape=jax.ShapeDtypeStruct((KEPT, ORB, LANES), F32),
        in_specs=[pl.BlockSpec(memory_space=pltpu.VMEM)] * 2,
        out_specs=pl.BlockSpec(memory_space=pltpu.VMEM),
        scratch_shapes=[
            pltpu.VMEM((SLABS, ORB, LANES), F32),
            pltpu.VMEM((SLABS, ORB, LANES), F32),
        ],
        compiler_params=pltpu.CompilerParams(vmem_limit_bytes=32 << 20),
        name="retarded",
    )(gathered, small)


ENERGIES = 64


def lag_kernel(in_ref, out_ref, gl, gg):
    first = lane_of((ENERGIES, LANES)) < ORB
    for half in range(2):
        gl[half, pl.ds(ENERGIES, 8), :] = jnp.zeros((8, LANES), F32)

    def one(index, unused):
        slab = index // 2
        orbital = index % 2
        sums = []
        for half in range(2):
            for parity in range(2):
                base = (half * 2 + parity) * (32 * 9) + slab * 3
                gl[half, pl.ds(parity, 32, stride=2), :] = in_ref[
                    pl.ds(base + orbital, 32, stride=9), :
                ]
                gg[half, pl.ds(parity, 32, stride=2), :] = in_ref[pl.ds(base + 2, 32, stride=9), :]
            power = gg[half]
            turned = pltpu.roll(power, ORB, 1)
            low = jnp.where(first, power, turned)
            high = jnp.where(first, turned, power)
            gg[half] = jnp.where(orbital == 0, low, high)
            acc = [jnp.zeros((8, LANES), F32) for _ in range(8)]
            for energy in range(ENERGIES):
                weight = jnp.broadcast_to(gg[half, energy : energy + 1, :], (8, LANES))
                for block in range((ENERGIES - energy + 7) // 8):
                    acc[block] = acc[block] + weight * gl[half, pl.ds(energy + 8 * block, 8), :]
            sums.append(jnp.concatenate(acc, axis=0))
        zero_turned = pltpu.roll(sums[0], ORB, 1)
        one_turned = pltpu.roll(sums[1], ORB, 1)
        scale = 1.0 / ENERGIES
        out_ref[pl.ds(index, ENERGIES, stride=6), :] = jnp.where(first, sums[0], one_turned) * scale
        out_ref[pl.ds(ENERGIES * 6 + index, ENERGIES, stride=6), :] = (
            jnp.where(first, zero_turned, sums[1]) * scale
        )
        return unused

    lax.fori_loop(0, 6, one, 0, unroll=True)


def correlate(received):
    return pl.pallas_call(
        lag_kernel,
        out_shape=jax.ShapeDtypeStruct((2 * ENERGIES * 6, LANES), F32),
        in_specs=[pl.BlockSpec(memory_space=pltpu.VMEM)],
        out_specs=pl.BlockSpec(memory_space=pltpu.VMEM),
        scratch_shapes=[
            pltpu.VMEM((2, ENERGIES + 8, LANES), F32),
            pltpu.VMEM((2, ENERGIES, LANES), F32),
        ],
        compiler_params=pltpu.CompilerParams(vmem_limit_bytes=32 << 20),
        name="lags",
    )(received)


GROUPS = 4
PER_GROUP = 32
LINK_ROWS = 3 * ORB
HALF_ROWS = LINK_ROWS // 2
PIECE_ROWS = LINK_ROWS + HALF_ROWS
MESH = pl.DeviceIdType.MESH


def gather_kernel(
    packed_ref, pair_ref, out_ref, small_ref,
    piece, small_piece, sent, arrived, passed, handed, small_sent, small_arrived,
):
    group = lax.axis_index("slab")
    spot = lax.axis_index("energy")
    core = lax.rem(spot, 2)
    sibling = spot + 1 - 2 * core
    barrier = pltpu.get_barrier_semaphore()
    for d in range(1, GROUPS):
        pl.semaphore_signal(
            barrier, inc=1, device_id=(lax.rem(group + d, GROUPS), spot), device_id_type=MESH
        )
    pl.semaphore_signal(barrier, inc=1, device_id=(group, sibling), device_id_type=MESH)
    my_half = group // 2

    first = lane_of((ORB, LANES)) < ORB
    for i in range(3):
        real, imag = packed_ref[i, 0, :, :LANES], packed_ref[i, 1, :, :LANES]
        p = jnp.where(first, real, pltpu.roll(imag, ORB, 1))
        q = jnp.where(first, pltpu.roll(real, ORB, 1), imag)
        span = pl.ds(i * ORB, ORB)
        out_ref[group, 0, span, :] = p
        out_ref[group, 1, span, :] = q
        mine = jnp.where(core == 0, p, q)
        piece[0, span, :] = mine
        piece[1, span, :] = mine
        real, imag = packed_ref[i, 0, :, LANES:], packed_ref[i, 1, :, LANES:]
        halves = (
            jnp.where(first, real, pltpu.roll(imag, ORB, 1)),
            jnp.where(first, pltpu.roll(real, ORB, 1), imag),
        )
        own = jnp.where(my_half == 0, halves[0], halves[1])
        for part in range(2):
            low = i * ORB + part * 32
            side, offset = divmod(low, HALF_ROWS)
            there = pl.ds(LINK_ROWS + offset, 32)
            rows = slice(part * 32, part * 32 + 32)
            out_ref[group, side, there, :] = own[rows]

            @pl.when(core == side)
            def _():
                piece[0, there, :] = halves[0][rows]
                piece[1, there, :] = halves[1][rows]

    pair = pair_ref[...]
    for parity in range(2):
        small_piece[parity, 0:3, :] = pair[:, parity]
    small_ref[group, 0:3, :] = jnp.where(lax.rem(group, 2) == 0, pair[:, 0], pair[:, 1])

    pl.semaphore_wait(barrier, GROUPS)
    smalls = []
    for d in (2, 1, 3):
        there = lax.rem(group + d, GROUPS)
        small = pltpu.make_async_remote_copy(
            src_ref=small_piece.at[lax.rem(there, 2)],
            dst_ref=small_ref.at[group],
            send_sem=small_sent.at[d],
            recv_sem=small_arrived.at[d],
            device_id=(there, spot),
            device_id_type=MESH,
        )
        small.start()
        smalls.append(small)
    def rows_at(chunk):
        return pl.ds(chunk * HALF_ROWS, HALF_ROWS)

    def to_group(chunk, d, there, source_ref, origin):
        return pltpu.make_async_remote_copy(
            src_ref=source_ref,
            dst_ref=out_ref.at[origin, core, rows_at(chunk)],
            send_sem=sent.at[chunk, d],
            recv_sem=arrived.at[chunk, d],
            device_id=(there, spot),
            device_id_type=MESH,
        )

    copies = {}
    for chunk, d in ((0, 1), (1, 3), (1, 1), (0, 3), (2, 2), (2, 1), (2, 3)):
        there = lax.rem(group + d, GROUPS)
        half = there // 2 if chunk == 2 else 0
        copies[chunk, d] = to_group(chunk, d, there, piece.at[half, rows_at(chunk)], group)
        copies[chunk, d].start()
    forwards = []
    for chunk, d in ((0, 1), (1, 3), (1, 1), (0, 3), (2, 1), (2, 3), (0, 2), (1, 2), (2, 2)):
        origin = lax.rem(group + GROUPS - d, GROUPS)
        copies[chunk, d].wait_recv()
        here = out_ref.at[origin, core, rows_at(chunk)]
        if (chunk, d) in ((0, 1), (1, 3)):
            copies[chunk, 2] = to_group(chunk, 2, lax.rem(group + d, GROUPS), here, origin)
            copies[chunk, 2].start()
        forward = pltpu.make_async_remote_copy(
            src_ref=here,
            dst_ref=here,
            send_sem=passed.at[chunk, d],
            recv_sem=handed.at[chunk, d],
            device_id=(group, sibling),
            device_id_type=MESH,
        )
        forward.start()
        forwards.append(forward)
    for small in smalls:
        small.wait()
    for copy in copies.values():
        copy.wait_send()
    for forward in forwards:
        forward.wait()


def gather_links(packed, pair):
    dma = pltpu.SemaphoreType.DMA
    return pl.pallas_call(
        gather_kernel,
        out_shape=(
            jax.ShapeDtypeStruct((GROUPS, 2, PIECE_ROWS, LANES), F32),
            jax.ShapeDtypeStruct((GROUPS, 8, LANES), F32),
        ),
        in_specs=[pl.BlockSpec(memory_space=pltpu.VMEM)] * 2,
        out_specs=[pl.BlockSpec(memory_space=pltpu.VMEM)] * 2,
        scratch_shapes=[
            pltpu.VMEM((2, PIECE_ROWS, LANES), F32),
            pltpu.VMEM((2, 8, LANES), F32),
            dma((3, GROUPS)),
            dma((3, GROUPS)),
            dma((3, GROUPS)),
            dma((3, GROUPS)),
            dma((GROUPS,)),
            dma((GROUPS,)),
        ],
        compiler_params=pltpu.CompilerParams(
            collective_id=0, has_side_effects=True, vmem_limit_bytes=16 << 20
        ),
        name="gather_links",
    )(packed, pair)


def exchange_kernel(kept, small_ref, out_ref, rhs, sol_ref, scratch, outgoing, sent, arrived, local):
    group = lax.axis_index("slab")
    spot = lax.axis_index("energy")
    here = group * PER_GROUP + spot
    count = GROUPS * PER_GROUP
    barrier = pltpu.get_barrier_semaphore()

    def greet(d, unused):
        there = lax.rem(here + d, count)
        pl.semaphore_signal(
            barrier,
            inc=1,
            device_id=(there // PER_GROUP, lax.rem(there, PER_GROUP)),
            device_id_type=MESH,
        )
        return unused

    def greet_eight(i, unused):
        for j in range(8):
            greet(1 + 8 * i + j, 0)
        return unused

    full = (count - 1) // 8
    lax.fori_loop(0, full, greet_eight, 0)
    for d in range(1 + 8 * full, count):
        greet(d, 0)

    corner = lane_of((ORB, LANES)) == row_of((ORB, LANES)) + ORB
    for s in range(SLABS):
        row = jnp.broadcast_to(small_ref[s // 3, s % 3 : s % 3 + 1, :], (ORB, LANES))
        gain = jnp.sum(jnp.where(corner, row, 0.0), axis=1, keepdims=True)
        rhs[s] = gain * kept[SOL + s]
    for level in LEVELS:
        for s, l, r in level:
            near = [n for n in (l, r) if n is not None]
            step = dot(kept[INV + s], right_form(rhs[s]))
            rhs[s] = step
            if not near:
                continue
            back = jnp.concatenate([kept[LINK + SLOTS[n, s]] for n in near], axis=0)
            moved = dot(back, right_form(step))
            for i, n in enumerate(near):
                rhs[n] = rhs[n] - moved[ORB * i : ORB * (i + 1)]

    def sol(s, value=None):
        if value is None:
            return sol_ref[s]
        sol_ref[s] = value

    climb(kept, rhs, sol)
    first = lane_of((ORB, LANES)) < ORB
    for s in range(SLABS):
        x, y = kept[SOL + s], sol_ref[s]
        same = x * y
        crossed = pltpu.roll(x, ORB, 1) * y
        turned = x * pltpu.roll(y, ORB, 1)
        square = x * x
        scratch[0, s] = jnp.where(first, same + pltpu.roll(same, ORB, 1), crossed - turned)
        scratch[1, s] = square + pltpu.roll(square, ORB, 1)
        there = pl.ds((s // 3) * PER_GROUP, PER_GROUP)
        low = (s % 3) * 3
        even = scratch[1, s, pl.ds(0, 32, stride=2), :]
        odd = scratch[1, s, pl.ds(1, 32, stride=2), :]
        outgoing[there, low, 0, :] = scratch[0, s, pl.ds(0, 32, stride=2), :]
        outgoing[there, low + 1, 0, :] = scratch[0, s, pl.ds(1, 32, stride=2), :]
        outgoing[there, low + 2, 0, :] = jnp.where(lane_of((32, LANES)) < ORB, even, odd)

    own = pltpu.make_async_copy(outgoing.at[here], out_ref.at[here], local)
    own.start()
    pl.semaphore_wait(barrier, count - 1)

    def send(there):
        pltpu.make_async_remote_copy(
            src_ref=outgoing.at[there],
            dst_ref=out_ref.at[here],
            send_sem=sent,
            recv_sem=arrived,
            device_id=(there // PER_GROUP, lax.rem(there, PER_GROUP)),
            device_id_type=MESH,
        ).start()

    z, x, core = spot // 8, lax.rem(spot // 2, 4), lax.rem(spot, 2)
    hops = (0, 1, 2, 1)
    planes = [(dy, dz) for dy in range(4) for dz in range(4)]
    planes.sort(key=lambda plane: -(hops[plane[0]] + hops[plane[1]]))
    for dy, dz in planes:
        plane = lax.rem(group + dy, 4) * PER_GROUP + lax.rem(z + dz, 4) * 8

        def spread_x(i, unused):
            dx = lax.rem(i // 2 + 2, 4)
            send(plane + lax.rem(x + dx, 4) * 2 + lax.rem(core + i, 2))
            return unused

        if (dy, dz) == (0, 0):
            for i in (0, 1, 2, 3, 6, 7, 5):
                spread_x(jnp.int32(i), 0)
        else:
            lax.fori_loop(0, 8, spread_x, 0, unroll=True)
    own.wait()
    others = pl.ds(0, count - 1)
    pltpu.make_async_copy(outgoing.at[others], outgoing.at[others], sent).wait()
    pltpu.make_async_copy(out_ref.at[others], out_ref.at[others], arrived).wait()


def lesser_and_exchange(kept, small):
    block = (GROUPS * PER_GROUP, 9, 1, LANES)
    return pl.pallas_call(
        exchange_kernel,
        out_shape=jax.ShapeDtypeStruct(block, F32),
        in_specs=[pl.BlockSpec(memory_space=pltpu.VMEM)] * 2,
        out_specs=pl.BlockSpec(memory_space=pltpu.VMEM),
        scratch_shapes=[
            pltpu.VMEM((SLABS, ORB, LANES), F32),
            pltpu.VMEM((SLABS, ORB, LANES), F32),
            pltpu.VMEM((2, SLABS, ORB, LANES), F32),
            pltpu.VMEM(block, F32),
            pltpu.SemaphoreType.DMA,
            pltpu.SemaphoreType.DMA,
            pltpu.SemaphoreType.DMA,
        ],
        compiler_params=pltpu.CompilerParams(
            collective_id=1, has_side_effects=True, vmem_limit_bytes=24 << 20
        ),
        name="lesser_and_exchange",
    )(kept, small)


def per_device(link_p, link_q, shift, lesser_gain, sources):
    packed = jnp.concatenate([link_p, link_q, sources], axis=-1)
    pair = jnp.swapaxes(jnp.concatenate([shift, lesser_gain], axis=-1), 0, 1)
    gathered, small = gather_links(packed, pair)
    kept = solve_retarded(gathered, small)
    received = lesser_and_exchange(kept, small)
    out = correlate(received.reshape(SLABS * 96, LANES))
    return out.reshape(2, ENERGIES, 3, 2, LANES)


def solution(mesh):
    placed = (
        P("slab", None, None, None),
        P("slab", None, None, None),
        P("energy", "slab", None),
        P("energy", "slab", None),
        P("slab", None, None, None),
    )
    return jax.shard_map(
        per_device,
        mesh=mesh,
        in_specs=placed,
        out_specs=P(None, None, "slab", "energy", None),
        check_vma=False,
    )
```
